512 devices in a mesh: angle: 16 (over z, y_hi), tile: 32 (over y_lo, x, core).
Axes of the slice: x: 4, y: 8 (y_hi: 2, y_lo: 4; y = y_hi * 4 + y_lo), z: 8, core: 2. Of those that a mesh axis runs over, the one named last changes fastest.
Arguments:
- volume: float32 [256, 2, 32, 256], P('tile'), may hold values from -1.8 to 1.8
- first_moment: float32 [256, 2, 32, 256], P('tile'), may hold values from -0.6 to 0.6
- second_moment: float32 [256, 2, 32, 256], P('tile'), may hold values from 0.01 to 0.1
- probe: float32 [2, 128, 128], replicated, may hold values from -6 to 6
- measured: bfloat16 [16, 32, 8, 128, 128], P('angle', 'tile'), may hold values from 0 to 2
- scan_rows: int32 [16, 32, 8], P('angle', 'tile'), may hold values from 0 to 128
- scan_cols: int32 [16, 32, 8], P('angle', 'tile'), may hold values from 0 to 256
- owner_ids: int32 [16, 32, 32], P('angle'), may hold values from 0 to 31, as said below
- block_ids: int32 [16, 32, 32], P('angle'), may hold values from 0 to 7
- interp_weights: float32 [16, 32, 16], P('angle', 'tile'), may hold values from 0 to 1
Outputs:
- new_volume: float32 [256, 2, 32, 256], P('tile')
- new_first: float32 [256, 2, 32, 256], P('tile')
- new_second: float32 [256, 2, 32, 256], P('tile')
The draws below stay inside these ranges and needn't reach their ends.
Inputs may be any that keep to these rules, and one draw needn't show every extreme that they name: `owner_ids`: among the 32 requests of one tile of one angle group, no owner is named more than 2 times, and one owner is named exactly 2 times.
All inputs are finite; a program needn't handle non-finite values.
Results may differ from the reference program's by a relative error of at most 0.0019.
Values may be sent and summed in bfloat16 or wider, within the bound.
A program may use at most 64 MiB of HBM per device.

```python
import math
import jax
import jax.numpy as jnp
from jax import lax

SLICE_WIDTH = 256
PROBE_WIDTH = 128
BLOCK_ROWS = 32
BLOCKS_DEV = 8
SLICES = 2
PROBES_DEV = 8
MARGIN = 64
BLOCKS_PER_SLICE = 8
ROW_BLOCKS = 16
REQUESTS = 32
CAPACITY = 2
VOLUME_BLOCKS = 256
N_ANGLE = 16
N_TILE = 32


def owner_row(row_key):
    perm_key, order_key = jax.random.split(row_key)
    favoured = jax.random.permutation(perm_key, N_TILE)
    request_slots = jnp.arange(REQUESTS, dtype=jnp.int32)
    position = jnp.where(request_slots < CAPACITY, 0, 1 + (request_slots - CAPACITY) % (N_TILE - 1))
    owners = favoured[position]
    order = jax.random.permutation(order_key, REQUESTS)
    return owners[order].astype(jnp.int32)


def draw_owner_ids(key, part):
    row_keys = jax.random.split(jax.random.fold_in(key, 11), N_ANGLE * N_TILE)
    return jax.vmap(owner_row)(row_keys).reshape(N_ANGLE, N_TILE, REQUESTS)


def set_ends(drawn, key, smallest, largest):
    longest = drawn.shape.index(max(drawn.shape))
    spots = []
    for shift in (0, 1):
        where = [jax.random.randint(jax.random.fold_in(key, axis), (), 0, length) for axis, length in enumerate(drawn.shape)]
        where[longest] = (where[longest] + shift) % drawn.shape[longest]
        spots.append(tuple(where))
    return drawn.at[spots[0]].set(smallest).at[spots[1]].set(largest)


def block_levels(key, dims, cuts, smallest, high):
    loudness = 1.0
    for axis_at, parts in cuts:
        heights = jax.random.uniform(jax.random.fold_in(jax.random.fold_in(key, 6), axis_at), (parts,), jnp.float32, smallest / len(cuts), high / len(cuts))
        loudness = loudness * jnp.repeat(jnp.exp(heights), dims[axis_at] // parts).reshape((-1,) + (1,) * (len(dims) - 1 - axis_at))
    return loudness


def normal_values(rng, shape, width, reach, cuts=(), held_as=jnp.bfloat16):
    level = block_levels(rng, shape, cuts, -0.22, 0.18) if cuts else 1.0
    drawn = jax.random.normal(rng, shape, jnp.float32) * width * level
    return jnp.minimum(jnp.maximum(drawn, -reach), reach).astype(held_as)


def setup_inputs(seed: int = 0) -> dict:
    seeds = jax.random.split(jax.random.key(seed), 11)
    return {
        "volume": normal_values(seeds[0], (VOLUME_BLOCKS, 2, BLOCK_ROWS, SLICE_WIDTH), 0.3, 1.8, ((0, 32),), jnp.float32),
        "first_moment": normal_values(seeds[1], (VOLUME_BLOCKS, 2, BLOCK_ROWS, SLICE_WIDTH), 0.1, 0.6, ((0, 32),), jnp.float32),
        "second_moment": jnp.clip(jnp.exp(math.log(0.1) - 2.3025851 * jax.random.uniform(seeds[2], (VOLUME_BLOCKS, 2, BLOCK_ROWS, SLICE_WIDTH), jnp.float32) ** block_levels(seeds[2], (VOLUME_BLOCKS, 2, BLOCK_ROWS, SLICE_WIDTH), ((0, 32),), -0.2, 0.2)), 0.01, 0.1),
        "probe": normal_values(seeds[3], (2, PROBE_WIDTH, PROBE_WIDTH), 1.0, 6.0, (), jnp.float32),
        "measured": jnp.clip(2.0 * jax.random.uniform(seeds[4], (N_ANGLE, N_TILE, PROBES_DEV, PROBE_WIDTH, PROBE_WIDTH), jnp.float32) ** block_levels(seeds[4], (N_ANGLE, N_TILE, PROBES_DEV, PROBE_WIDTH, PROBE_WIDTH), ((0, 16), (1, 32)), -0.2, 0.2), 0.0, 2.0).astype(jnp.bfloat16),
        "scan_rows": set_ends(jax.random.randint(seeds[5], (N_ANGLE, N_TILE, PROBES_DEV), 0, SLICE_WIDTH - PROBE_WIDTH + 1), jax.random.fold_in(seeds[5], 1), 0, SLICE_WIDTH - PROBE_WIDTH).astype(jnp.int32),
        "scan_cols": set_ends(jax.random.randint(seeds[6], (N_ANGLE, N_TILE, PROBES_DEV), 0, SLICE_WIDTH + 1), jax.random.fold_in(seeds[6], 1), 0, SLICE_WIDTH).astype(jnp.int32),
        "owner_ids": draw_owner_ids(jax.random.fold_in(seeds[10], 71), 0),
        "block_ids": set_ends(jax.random.randint(seeds[8], (N_ANGLE, N_TILE, REQUESTS), 0, BLOCKS_DEV), jax.random.fold_in(seeds[8], 1), 0, BLOCKS_DEV - 1).astype(jnp.int32),
        "interp_weights": jnp.clip(1.0 * jax.random.uniform(seeds[9], (N_ANGLE, N_TILE, ROW_BLOCKS), jnp.float32) ** block_levels(seeds[9], (N_ANGLE, N_TILE, ROW_BLOCKS), ((0, 16), (1, 32)), -0.2, 0.2), 0.0, 1.0),
    }


FRESNEL = 0.35
SMOOTHING = 0.25
BETA_FIRST = 0.9
BETA_SECOND = 0.999
STEP_SIZE = 0.05
EPSILON = 1e-08

def dft_tables(length):
    index = jnp.arange(length, dtype=jnp.int32)
    product = index[:, None] * index[None, :] % length
    angles = product.astype(jnp.float32) * (2.0 * math.pi / length)
    factor = 1.0 / math.sqrt(length)
    dft_real = jnp.cos(angles) * factor
    dft_imag = -jnp.sin(angles) * factor
    signed = jnp.where(index < length // 2, index, index - length)
    squared = (signed * signed).astype(jnp.float32)
    phase = (squared[:, None] + squared[None, :]) * (-2.0 * math.pi * FRESNEL / length)
    return (dft_real, dft_imag, jnp.cos(phase), jnp.sin(phase))

def complex_matmul(left_real, left_imag, right_real, right_imag):
    highest = lax.Precision.HIGHEST
    out_real = jnp.dot(left_real, right_real, precision=highest) - jnp.dot(left_imag, right_imag, precision=highest)
    out_imag = jnp.dot(left_real, right_imag, precision=highest) + jnp.dot(left_imag, right_real, precision=highest)
    return (out_real, out_imag)

def transform(field_real, field_imag, table_real, table_imag):
    half_real, half_imag = complex_matmul(table_real, table_imag, field_real, field_imag)
    return complex_matmul(half_real, half_imag, table_real, table_imag)

def probe_loss(object_pad, probe, start_row, start_col, amplitude, tables):
    dft_real, dft_imag, kernel_real, kernel_imag = tables
    probe_size = probe.shape[-1]
    layers = object_pad.shape[0]
    anchor = jnp.zeros((), jnp.int32)
    starts = (anchor, anchor, start_row.astype(jnp.int32), start_col.astype(jnp.int32))
    window = lax.dynamic_slice(object_pad, starts, (layers, 2, probe_size, probe_size))
    wave_real = probe[0]
    wave_imag = probe[1]
    for layer_index in range(layers):
        trans_real = 1.0 + window[layer_index, 0]
        trans_imag = window[layer_index, 1]
        wave_real, wave_imag = (wave_real * trans_real - wave_imag * trans_imag, wave_real * trans_imag + wave_imag * trans_real)
        if layer_index + 1 < layers:
            spec_real, spec_imag = transform(wave_real, wave_imag, dft_real, dft_imag)
            spec_real, spec_imag = (spec_real * kernel_real - spec_imag * kernel_imag, spec_real * kernel_imag + spec_imag * kernel_real)
            wave_real, wave_imag = transform(spec_real, spec_imag, dft_real, -dft_imag)
    far_real, far_imag = transform(wave_real, wave_imag, dft_real, dft_imag)
    modulus = jnp.sqrt(far_real * far_real + far_imag * far_imag + SMOOTHING)
    misfit = modulus - amplitude.astype(jnp.float32)
    return 0.5 * jnp.sum(misfit * misfit)

def local_gradient(padded, probe, rows_list, cols_list, amplitudes, tables):

    def total_loss(object_pad):

        def single(start_row, start_col, amplitude):
            return probe_loss(object_pad, probe, start_row, start_col, amplitude, tables)
        return jnp.sum(jax.vmap(single)(rows_list, cols_list, amplitudes))
    value, pullback = jax.vjp(total_loss, padded)
    return pullback(jnp.ones((), padded.dtype))[0]

def adam_update(params, moment_one, moment_two, gradient):
    fresh_one = BETA_FIRST * moment_one + (1.0 - BETA_FIRST) * gradient
    fresh_two = BETA_SECOND * moment_two + (1.0 - BETA_SECOND) * gradient * gradient
    fresh_params = params - STEP_SIZE * fresh_one / (jnp.sqrt(fresh_two) + EPSILON)
    return (fresh_params, fresh_one, fresh_two)

def reference(volume, first_moment, second_moment, probe, measured, scan_rows, scan_cols, owner_ids, block_ids, interp_weights):
    blocks = volume.astype(jnp.bfloat16)
    tables = dft_tables(PROBE_WIDTH)
    tile_gradient = jax.vmap(local_gradient, in_axes=(0, None, 0, 0, 0, None))

    def angle_term(running, angle_index):
        source = owner_ids[angle_index] * BLOCKS_DEV + block_ids[angle_index]
        weight = interp_weights[angle_index][:, :, None, None, None]
        complement = 1.0 - weight
        fetched = blocks[source].astype(jnp.float32).reshape(N_TILE, ROW_BLOCKS, 2, 2, BLOCK_ROWS, SLICE_WIDTH)
        obj_rows = weight * fetched[:, :, 0] + complement * fetched[:, :, 1]
        object_tiles = obj_rows.reshape(N_TILE, SLICES, BLOCKS_PER_SLICE, 2, BLOCK_ROWS, SLICE_WIDTH)
        object_tiles = object_tiles.transpose(0, 1, 3, 2, 4, 5).reshape(N_TILE, SLICES, 2, SLICE_WIDTH, SLICE_WIDTH)
        object_tiles = object_tiles.astype(jnp.bfloat16)
        empty = jnp.zeros_like(object_tiles[:1])
        before = jnp.concatenate([empty, object_tiles[:-1]], axis=0)
        after = jnp.concatenate([object_tiles[1:], empty], axis=0)
        padded = jnp.concatenate([before[..., SLICE_WIDTH - MARGIN:], object_tiles, after[..., :MARGIN]], axis=-1)
        padded = padded.astype(jnp.float32)
        grad_padded = tile_gradient(padded, probe, scan_rows[angle_index], scan_cols[angle_index], measured[angle_index], tables)
        empty_grad = jnp.zeros_like(grad_padded[:1])
        from_left = jnp.concatenate([empty_grad, grad_padded[:-1]], axis=0)[..., MARGIN + SLICE_WIDTH:]
        from_right = jnp.concatenate([grad_padded[1:], empty_grad], axis=0)[..., :MARGIN]
        interior = grad_padded[..., MARGIN:MARGIN + SLICE_WIDTH]
        interior = interior.at[..., :MARGIN].add(from_left)
        interior = interior.at[..., SLICE_WIDTH - MARGIN:].add(from_right)
        grad_rows = interior.reshape(N_TILE, SLICES, 2, BLOCKS_PER_SLICE, BLOCK_ROWS, SLICE_WIDTH)
        grad_rows = grad_rows.transpose(0, 1, 3, 2, 4, 5).reshape(N_TILE, ROW_BLOCKS, 2, BLOCK_ROWS, SLICE_WIDTH)
        request_grads = jnp.stack([weight * grad_rows, complement * grad_rows], axis=2)
        request_grads = request_grads.reshape(N_TILE * REQUESTS, 2, BLOCK_ROWS, SLICE_WIDTH).astype(jnp.bfloat16)
        request_grads = lax.optimization_barrier(request_grads).astype(jnp.float32)
        summed = jax.ops.segment_sum(request_grads, source.reshape(-1), num_segments=VOLUME_BLOCKS)
        return (running + summed, None)
    initial = jnp.zeros(volume.shape, jnp.float32)
    grad_volume, ignored = lax.scan(angle_term, initial, jnp.arange(N_ANGLE, dtype=jnp.int32))
    fresh_params, fresh_one, fresh_two = adam_update(volume, first_moment, second_moment, grad_volume)
    return (fresh_params, fresh_one, fresh_two)
```

```python
import math

import jax
import jax.numpy as jnp
import numpy as np
from jax import lax
from jax.experimental import pallas as pl
from jax.experimental.pallas import tpu as pltpu
from jax.sharding import PartitionSpec as P

FRESNEL = 0.35
SMOOTHING = 0.25
BETA_FIRST = 0.9
BETA_SECOND = 0.999
STEP_SIZE = 0.05
EPSILON = 1e-08


def with_halo(cells, sides, width):
    for axis, dim in sides:
        count = lax.axis_size(axis)
        ends = count - 1
        head = lax.slice_in_dim(cells, 0, width, axis=dim)
        tail = lax.slice_in_dim(cells, cells.shape[dim] - width, cells.shape[dim], axis=dim)
        cells = jnp.concatenate(
            [
                lax.ppermute(tail, axis, [(i, (i + 1) % count) for i in range(ends)]),
                cells,
                lax.ppermute(head, axis, [((i + 1) % count, i) for i in range(ends)]),
            ],
            axis=dim,
        )
    return cells


def from_behind(array, axis, by):
    length = lax.axis_size(axis)
    pairs = [(i, i + by) for i in range(length) if 0 <= i + by < length]
    return lax.ppermute(array, axis, pairs)


def block_form(table):
    real = np.concatenate([np.concatenate([table.real, table.imag], 1),
                           np.concatenate([-table.imag, table.real], 1)], 0)
    real = real.astype(np.float32)
    head = real.astype(jnp.bfloat16)
    rest = (real - head.astype(np.float32)).astype(jnp.bfloat16)
    return head, rest


def operator_tables(length):
    index = np.arange(length)
    table = np.exp(-2j * np.pi * (np.outer(index, index) % length) / length) / math.sqrt(length)
    signed = np.where(index < length // 2, index, index - length)
    phase = np.exp(-2j * np.pi * FRESNEL * signed * signed / length)
    step = (table.conj() * phase[None, :]) @ table
    out = []
    for operator in (table, step):
        out += [*block_form(operator), *block_form(operator.conj())]
    return np.stack(out)


def split_bf16(x):
    head = x.astype(jnp.bfloat16)
    return head, (x - head.astype(jnp.float32)).astype(jnp.bfloat16)


def mm(a, b):
    return jnp.dot(a, b, preferred_element_type=jnp.float32)


def wave_kernel(size, chunk, rows_ref, cols_ref, obj_ref, probe_ref, amp_ref, tab_ref, acc_ref):
    probes = amp_ref.shape[0]
    n = size

    def two_sided(real, imag, right, left):
        stacked = jnp.concatenate([jnp.concatenate([r, i], 1) for r, i in zip(real, imag)], 0)
        head, rest = split_bf16(stacked)
        half = mm(head, tab_ref[right]) + (mm(rest, tab_ref[right]) + mm(head, tab_ref[right + 1]))
        out_real, out_imag = [], []
        for k in range(0, len(real), 2):
            one = half[k * n : (k + 1) * n]
            two = half[(k + 1) * n : (k + 2) * n]
            pair = jnp.concatenate(
                [jnp.concatenate([one[:, :n], two[:, :n]], 1),
                 jnp.concatenate([one[:, n:], two[:, n:]], 1)], 0)
            head, rest = split_bf16(pair)
            full = mm(tab_ref[left], head) + (mm(tab_ref[left], rest) + mm(tab_ref[left + 1], head))
            out_real += [full[:n, :n], full[:n, n:]]
            out_imag += [full[n:, :n], full[n:, n:]]
        return out_real, out_imag

    acc_ref[...] = jnp.zeros_like(acc_ref)
    p_real = probe_ref[0]
    p_imag = probe_ref[1]

    def body(step, carry):
        first = step * chunk
        place, trans = [], []
        for k in range(chunk):
            row = rows_ref[0, first + k]
            col = cols_ref[0, first + k]
            base = pl.multiple_of(jnp.minimum(col // n, 1) * n, n)
            shift = col - base
            top = pl.multiple_of(jnp.minimum(row // 8, n // 8 - 1) * 8, 8)
            down = row - top
            place.append((top, down, base, shift))
            back = lax.rem(2 * n - shift, 2 * n)
            up = lax.rem(n + 8 - down, n + 8)
            window = []
            for c in range(4):
                wide = obj_ref[c, pl.ds(top, n + 8), pl.ds(base, 2 * n)]
                part = pltpu.roll(pltpu.roll(wide, back, 1)[:, :n], up, 0)[:n]
                window.append(part + 1.0 if c % 2 == 0 else part)
            trans.append(window)
        w_real = [p_real * t[0] - p_imag * t[1] for t in trans]
        w_imag = [p_real * t[1] + p_imag * t[0] for t in trans]
        u_real, u_imag = two_sided(w_real, w_imag, 4, 6)
        w_real = [r * t[2] - i * t[3] for r, i, t in zip(u_real, u_imag, trans)]
        w_imag = [r * t[3] + i * t[2] for r, i, t in zip(u_real, u_imag, trans)]
        f_real, f_imag = two_sided(w_real, w_imag, 0, 2)
        g_real, g_imag = [], []
        for k in range(chunk):
            r, i = f_real[k], f_imag[k]
            scale = 1.0 - amp_ref[first + k].astype(jnp.float32) * lax.rsqrt(r * r + i * i + SMOOTHING)
            g_real.append(r * scale)
            g_imag.append(i * scale)
        g_real, g_imag = two_sided(g_real, g_imag, 2, 0)
        d_real = [u * r + v * i for u, v, r, i in zip(u_real, u_imag, g_real, g_imag)]
        d_imag = [u * i - v * r for u, v, r, i in zip(u_real, u_imag, g_real, g_imag)]
        b_real = [t[2] * r + t[3] * i for t, r, i in zip(trans, g_real, g_imag)]
        b_imag = [t[2] * i - t[3] * r for t, r, i in zip(trans, g_real, g_imag)]
        b_real, b_imag = two_sided(b_real, b_imag, 6, 4)
        for k in range(chunk):
            r, i = b_real[k], b_imag[k]
            parts = (p_real * r + p_imag * i, p_real * i - p_imag * r, d_real[k], d_imag[k])
            top, down, base, shift = place[k]
            for c in range(4):
                tall = jnp.concatenate([parts[c], jnp.zeros((8, n), jnp.float32)], 0)
                tall = pltpu.roll(tall, down, 0)
                wide = jnp.concatenate([tall, jnp.zeros_like(tall)], 1)
                wide = pltpu.roll(wide, shift, 1)
                acc_ref[c, pl.ds(top, n + 8), pl.ds(base, 2 * n)] += wide
        return carry

    lax.fori_loop(0, probes // chunk, body, 0)


def local_gradient(padded, probe, rows_list, cols_list, amplitudes):
    layers, parts, high, wide = padded.shape
    size = probe.shape[-1]
    probes = amplitudes.shape[0]
    chunk = 4 if probes % 4 == 0 else 2
    tables = jnp.asarray(operator_tables(size))
    smem = pl.BlockSpec(memory_space=pltpu.SMEM)
    vmem = pl.BlockSpec(memory_space=pltpu.VMEM)
    out = pl.pallas_call(
        lambda *refs: wave_kernel(size, chunk, *refs),
        out_shape=jax.ShapeDtypeStruct((layers * parts, high, wide), jnp.float32),
        in_specs=[smem, smem, vmem, vmem, vmem, vmem],
        out_specs=vmem,
        name="waves",
    )(
        rows_list.reshape(1, -1),
        cols_list.reshape(1, -1),
        padded.reshape(layers * parts, high, wide),
        probe,
        amplitudes,
        tables,
    )
    return out.reshape(layers, parts, high, wide)


def adam_update(params, moment_one, moment_two, gradient):
    fresh_one = BETA_FIRST * moment_one + (1.0 - BETA_FIRST) * gradient
    fresh_two = BETA_SECOND * moment_two + (1.0 - BETA_SECOND) * gradient * gradient
    fresh_params = params - STEP_SIZE * fresh_one / (jnp.sqrt(fresh_two) + EPSILON)
    return (fresh_params, fresh_one, fresh_two)


def per_device(
    volume,
    first_moment,
    second_moment,
    probe,
    measured,
    scan_rows,
    scan_cols,
    owner_ids,
    block_ids,
    interp_weights,
):
    tile_index = lax.axis_index("tile")
    tile_count = lax.axis_size("tile")
    block_count = volume.shape[0]
    block_rows = volume.shape[2]
    slab_width = volume.shape[3]
    probe_size = probe.shape[1]
    margin = probe_size // 2
    requests = owner_ids.shape[2]
    row_blocks = interp_weights.shape[2]
    per_slice = slab_width // block_rows
    layers = row_blocks // per_slice
    capacity = max(2, requests // tile_count)
    group_owner = owner_ids[0]
    group_block = block_ids[0]
    request_slots = jnp.arange(requests, dtype=jnp.int32)
    earlier = request_slots[None, :] < request_slots[:, None]
    same_owner = group_owner[:, :, None] == group_owner[:, None, :]
    group_rank = jnp.sum(same_owner & earlier[None], axis=2)
    my_owner = lax.dynamic_index_in_dim(group_owner, tile_index, 0, keepdims=False)
    my_rank = lax.dynamic_index_in_dim(group_rank, tile_index, 0, keepdims=False)
    slot_ids = jnp.arange(capacity, dtype=jnp.int32)
    serving = (group_owner == tile_index)[:, None, :] & (
        group_rank[:, None, :] == slot_ids[None, :, None]
    )
    send_block = jnp.sum(jnp.where(serving, group_block[:, None, :], 0), axis=2)
    send_valid = jnp.any(serving, axis=2)
    blocks = volume.astype(jnp.bfloat16)
    weight = interp_weights[0, 0]
    complement = 1.0 - weight
    outgoing = jnp.where(
        send_valid[:, :, None, None, None], blocks[send_block], jnp.zeros((), jnp.bfloat16)
    )
    incoming = lax.all_to_all(outgoing, "tile", split_axis=0, concat_axis=0, tiled=True)
    fetched = (
        incoming[my_owner, my_rank]
        .astype(jnp.float32)
        .reshape(row_blocks, 2, 2, block_rows, slab_width)
    )
    obj_rows = (
        weight[:, None, None, None] * fetched[:, 0]
        + complement[:, None, None, None] * fetched[:, 1]
    )
    object_tile = obj_rows.reshape(layers, per_slice, 2, block_rows, slab_width).transpose(
        0, 2, 1, 3, 4
    )
    object_tile = object_tile.reshape(layers, 2, slab_width, slab_width).astype(jnp.bfloat16)
    padded = with_halo(object_tile, (("tile", 3),), margin).astype(jnp.float32)
    grad_padded = local_gradient(padded, probe, scan_rows[0, 0], scan_cols[0, 0], measured[0, 0])
    edges = grad_padded.astype(jnp.bfloat16)
    from_left = from_behind(edges[..., margin + slab_width :], "tile", 1).astype(jnp.float32)
    from_right = from_behind(edges[..., :margin], "tile", -1).astype(jnp.float32)
    interior = grad_padded[..., margin : margin + slab_width]
    middle = jnp.zeros((layers, 2, slab_width, slab_width - 2 * margin), jnp.float32)
    interior = interior + jnp.concatenate([from_left, middle, from_right], axis=3)
    grad_rows = interior.reshape(layers, 2, per_slice, block_rows, slab_width).transpose(
        0, 2, 1, 3, 4
    )
    grad_rows = grad_rows.reshape(row_blocks, 2, block_rows, slab_width)
    request_grads = jnp.stack(
        [weight[:, None, None, None] * grad_rows, complement[:, None, None, None] * grad_rows],
        axis=1,
    )
    request_grads = request_grads.reshape(requests, 2, block_rows, slab_width).astype(jnp.bfloat16)
    owner_range = jnp.arange(tile_count, dtype=jnp.int32)
    owned_slots = (my_owner[None, None, :] == owner_range[:, None, None]) & (
        my_rank[None, None, :] == slot_ids[None, :, None]
    )
    back_index = jnp.sum(jnp.where(owned_slots, request_slots[None, None, :], 0), axis=2)
    back_valid = jnp.any(owned_slots, axis=2)
    returning = jnp.where(
        back_valid[:, :, None, None, None], request_grads[back_index], jnp.zeros((), jnp.bfloat16)
    )
    arrived = lax.all_to_all(returning, "tile", split_axis=0, concat_axis=0, tiled=True)
    selector = (
        send_block[:, :, None] == jnp.arange(block_count, dtype=jnp.int32)[None, None, :]
    ) & send_valid[:, :, None]
    selector = selector.reshape(tile_count * capacity, block_count).astype(jnp.bfloat16)
    grad_volume = jnp.einsum(
        "nb,nx->bx",
        selector,
        arrived.reshape(tile_count * capacity, -1),
        preferred_element_type=jnp.float32,
    ).reshape(volume.shape)
    rows_total = block_count * 2 * block_rows
    angles = lax.axis_size("angle")
    partial_sums = grad_volume.reshape(angles, rows_total // angles, slab_width)
    parts = lax.all_to_all(partial_sums.astype(jnp.bfloat16), "angle", 0, 0, tiled=True)
    share = jnp.sum(parts.astype(jnp.float32), axis=0)
    spread = jnp.broadcast_to(share[None], (angles, *share.shape))
    gradient = lax.all_to_all(spread, "angle", 0, 0, tiled=True).reshape(volume.shape)
    return adam_update(volume, first_moment, second_moment, gradient)


def solution(mesh):
    in_specs = (
        P("tile", None, None, None),
        P("tile", None, None, None),
        P("tile", None, None, None),
        P(),
        P("angle", "tile", None, None, None),
        P("angle", "tile", None),
        P("angle", "tile", None),
        P("angle", None, None),
        P("angle", None, None),
        P("angle", "tile", None),
    )
    out_specs = (
        P("tile", None, None, None),
        P("tile", None, None, None),
        P("tile", None, None, None),
    )
    return jax.shard_map(
        per_device, mesh=mesh, in_specs=in_specs, out_specs=out_specs, check_vma=False
    )
```

```python
import math

import jax
import jax.numpy as jnp
import numpy as np
from jax import lax
from jax.experimental import pallas as pl
from jax.experimental.pallas import tpu as pltpu
from jax.sharding import PartitionSpec as P

FRESNEL = 0.35
SMOOTHING = 0.25
BETA_FIRST = 0.9
BETA_SECOND = 0.999
STEP_SIZE = 0.05
EPSILON = 1e-08


def with_halo(cells, sides, width):
    for axis, dim in sides:
        count = lax.axis_size(axis)
        ends = count - 1
        head = lax.slice_in_dim(cells, 0, width, axis=dim)
        tail = lax.slice_in_dim(cells, cells.shape[dim] - width, cells.shape[dim], axis=dim)
        cells = jnp.concatenate(
            [
                lax.ppermute(tail, axis, [(i, (i + 1) % count) for i in range(ends)]),
                cells,
                lax.ppermute(head, axis, [((i + 1) % count, i) for i in range(ends)]),
            ],
            axis=dim,
        )
    return cells


def from_behind(array, axis, by):
    length = lax.axis_size(axis)
    pairs = [(i, i + by) for i in range(length) if 0 <= i + by < length]
    return lax.ppermute(array, axis, pairs)


def block_form(table):
    real = np.concatenate([np.concatenate([table.real, table.imag], 1),
                           np.concatenate([-table.imag, table.real], 1)], 0)
    real = real.astype(np.float32)
    head = real.astype(jnp.bfloat16)
    rest = (real - head.astype(np.float32)).astype(jnp.bfloat16)
    return head, rest


def operator_tables(length):
    index = np.arange(length)
    table = np.exp(-2j * np.pi * (np.outer(index, index) % length) / length) / math.sqrt(length)
    signed = np.where(index < length // 2, index, index - length)
    phase = np.exp(-2j * np.pi * FRESNEL * signed * signed / length)
    step = (table.conj() * phase[None, :]) @ table
    out = []
    for operator in (table, step):
        out += [*block_form(operator), *block_form(operator.conj())]
    return np.stack(out)


def split_bf16(x):
    head = x.astype(jnp.bfloat16)
    return head, (x - head.astype(jnp.float32)).astype(jnp.bfloat16)


def mm(a, b):
    return jnp.dot(a, b, preferred_element_type=jnp.float32)


def wave_kernel(size, chunk, rows_ref, cols_ref, obj_ref, probe_ref, amp_ref, tab_ref, acc_ref):
    probes = amp_ref.shape[0]
    n = size

    def two_sided(real, imag, right, left):
        stacked = jnp.concatenate([jnp.concatenate([r, i], 1) for r, i in zip(real, imag)], 0)
        head, rest = split_bf16(stacked)
        half = mm(head, tab_ref[right]) + (mm(rest, tab_ref[right]) + mm(head, tab_ref[right + 1]))
        out_real, out_imag = [], []
        for k in range(0, len(real), 2):
            one = half[k * n : (k + 1) * n]
            two = half[(k + 1) * n : (k + 2) * n]
            pair = jnp.concatenate(
                [jnp.concatenate([one[:, :n], two[:, :n]], 1),
                 jnp.concatenate([one[:, n:], two[:, n:]], 1)], 0)
            head, rest = split_bf16(pair)
            full = mm(tab_ref[left], head) + (mm(tab_ref[left], rest) + mm(tab_ref[left + 1], head))
            out_real += [full[:n, :n], full[:n, n:]]
            out_imag += [full[n:, :n], full[n:, n:]]
        return out_real, out_imag

    acc_ref[...] = jnp.zeros_like(acc_ref)
    p_real = probe_ref[0]
    p_imag = probe_ref[1]

    def body(step, carry):
        first = step * chunk
        place, trans = [], []
        for k in range(chunk):
            row = rows_ref[0, first + k]
            col = cols_ref[0, first + k]
            base = pl.multiple_of(jnp.minimum(col // n, 1) * n, n)
            shift = col - base
            top = pl.multiple_of(jnp.minimum(row // 8, n // 8 - 1) * 8, 8)
            down = row - top
            place.append((top, down, base, shift))
            back = lax.rem(2 * n - shift, 2 * n)
            up = lax.rem(n + 8 - down, n + 8)
            window = []
            for c in range(4):
                wide = obj_ref[c, pl.ds(top, n + 8), pl.ds(base, 2 * n)]
                part = pltpu.roll(pltpu.roll(wide, back, 1)[:, :n], up, 0)[:n]
                window.append(part + 1.0 if c % 2 == 0 else part)
            trans.append(window)
        w_real = [p_real * t[0] - p_imag * t[1] for t in trans]
        w_imag = [p_real * t[1] + p_imag * t[0] for t in trans]
        u_real, u_imag = two_sided(w_real, w_imag, 4, 6)
        w_real = [r * t[2] - i * t[3] for r, i, t in zip(u_real, u_imag, trans)]
        w_imag = [r * t[3] + i * t[2] for r, i, t in zip(u_real, u_imag, trans)]
        f_real, f_imag = two_sided(w_real, w_imag, 0, 2)
        g_real, g_imag = [], []
        for k in range(chunk):
            r, i = f_real[k], f_imag[k]
            scale = 1.0 - amp_ref[first + k].astype(jnp.float32) * lax.rsqrt(r * r + i * i + SMOOTHING)
            g_real.append(r * scale)
            g_imag.append(i * scale)
        g_real, g_imag = two_sided(g_real, g_imag, 2, 0)
        d_real = [u * r + v * i for u, v, r, i in zip(u_real, u_imag, g_real, g_imag)]
        d_imag = [u * i - v * r for u, v, r, i in zip(u_real, u_imag, g_real, g_imag)]
        b_real = [t[2] * r + t[3] * i for t, r, i in zip(trans, g_real, g_imag)]
        b_imag = [t[2] * i - t[3] * r for t, r, i in zip(trans, g_real, g_imag)]
        b_real, b_imag = two_sided(b_real, b_imag, 6, 4)
        for k in range(chunk):
            r, i = b_real[k], b_imag[k]
            parts = (p_real * r + p_imag * i, p_real * i - p_imag * r, d_real[k], d_imag[k])
            top, down, base, shift = place[k]
            for c in range(4):
                tall = jnp.concatenate([parts[c], jnp.zeros((8, n), jnp.float32)], 0)
                tall = pltpu.roll(tall, down, 0)
                wide = jnp.concatenate([tall, jnp.zeros_like(tall)], 1)
                wide = pltpu.roll(wide, shift, 1)
                acc_ref[c, pl.ds(top, n + 8), pl.ds(base, 2 * n)] += wide
        return carry

    lax.fori_loop(0, probes // chunk, body, 0)


def local_gradient(padded, probe, rows_list, cols_list, amplitudes):
    layers, parts, high, wide = padded.shape
    size = probe.shape[-1]
    probes = amplitudes.shape[0]
    chunk = 4 if probes % 4 == 0 else 2
    tables = jnp.asarray(operator_tables(size))
    smem = pl.BlockSpec(memory_space=pltpu.SMEM)
    vmem = pl.BlockSpec(memory_space=pltpu.VMEM)
    out = pl.pallas_call(
        lambda *refs: wave_kernel(size, chunk, *refs),
        out_shape=jax.ShapeDtypeStruct((layers * parts, high, wide), jnp.float32),
        in_specs=[smem, smem, vmem, vmem, vmem, vmem],
        out_specs=vmem,
        name="waves",
    )(
        rows_list.reshape(1, -1),
        cols_list.reshape(1, -1),
        padded.reshape(layers * parts, high, wide),
        probe,
        amplitudes,
        tables,
    )
    return out.reshape(layers, parts, high, wide)


MESH = pl.DeviceIdType.MESH


def place(tile, across):
    return tile % 2, tile // 2 % across, tile // (2 * across)


def greet(axis):
    count = lax.axis_size(axis)
    me = lax.axis_index(axis)
    barrier = pltpu.get_barrier_semaphore()

    def signal(d, carry):
        pl.semaphore_signal(
            barrier, inc=1, device_id={axis: lax.rem(me + d, count)}, device_id_type=MESH
        )
        return carry

    lax.fori_loop(1, count, signal, 0)
    pl.semaphore_wait(barrier, count - 1)


def direct_copy(d, source, target, send_sem, recv_sem):
    count = lax.axis_size("tile")
    me = lax.axis_index("tile")
    peer = lax.rem(me + d, count)
    return pltpu.make_async_remote_copy(
        src_ref=source.at[peer],
        dst_ref=target.at[me],
        send_sem=send_sem.at[d],
        recv_sem=recv_sem.at[d],
        device_id={"tile": peer},
        device_id_type=MESH,
    )


def start_direct(source, target, own_sem, send_sem, recv_sem):
    me = lax.axis_index("tile")
    own = pltpu.make_async_copy(source.at[me], target.at[me], own_sem)
    own.start()

    def start(d, carry):
        direct_copy(d, source, target, send_sem, recv_sem).start()
        return carry

    lax.fori_loop(1, lax.axis_size("tile"), start, 0)
    return own


def wait_direct(source, target, send_sem, recv_sem):
    def wait(d, carry):
        direct_copy(d, source, target, send_sem, recv_sem).wait()
        return carry

    lax.fori_loop(1, lax.axis_size("tile"), wait, 0)


def fetch_kernel(across, rows, direct, extra, got, near, near_sum, run, run_sum, far,
                 own_sem, send_sem, recv_sem, hop_send, hop_recv):
    count = lax.axis_size("tile")
    core, col, row = place(lax.axis_index("tile"), across)

    def hop(k, source, target, tile):
        return pltpu.make_async_remote_copy(
            src_ref=source, dst_ref=target, send_sem=hop_send.at[k], recv_sem=hop_recv.at[k],
            device_id={"tile": tile}, device_id_type=MESH)

    greet("tile")
    first = hop(0, extra.at[1 - core], near, (row * across + col) * 2 + 1 - core)
    first.start()
    first.wait()
    near_sum[...] = extra[core] + near[...]
    hops = []
    for k in range(1, across):
        to = lax.rem(col + k, across)
        hops.append(hop(k, near_sum.at[to], run.at[k - 1], (row * across + to) * 2 + core))
        hops[-1].start()
    own = start_direct(direct, got, own_sem, send_sem, recv_sem)
    for copy in hops:
        copy.wait()
    total = near_sum[col]
    for k in range(across - 1):
        total = total + run[k]
    run_sum[...] = total
    hops = []
    for k in range(1, rows):
        to = lax.rem(row + k, rows)
        hops.append(hop(across - 1 + k, run_sum.at[to], far.at[k - 1], (to * across + col) * 2 + core))
        hops[-1].start()
    for copy in hops:
        copy.wait()
    total = run_sum[row]
    for k in range(rows - 1):
        total = total + far[k]
    got[count] = total
    own.wait()
    wait_direct(direct, got, send_sem, recv_sem)


def return_kernel(across, rows, direct, extra, got,
                  own_sem, send_sem, recv_sem, hop_send, hop_recv):
    count = lax.axis_size("tile")
    core, col, row = place(lax.axis_index("tile"), across)
    half = across * rows

    def hop(k, source, target, tile):
        return pltpu.make_async_remote_copy(
            src_ref=source, dst_ref=target, send_sem=hop_send.at[k], recv_sem=hop_recv.at[k],
            device_id={"tile": tile}, device_id_type=MESH)

    greet("tile")
    base = count + core * half + col * rows
    mine = pltpu.make_async_copy(extra, got.at[base + row], hop_send.at[across + rows - 1])
    mine.start()
    hops = []
    for k in range(1, rows):
        to = lax.rem(row + k, rows)
        hops.append(hop(k, extra, got.at[base + row], (to * across + col) * 2 + core))
        hops[-1].start()
    own = start_direct(direct, got, own_sem, send_sem, recv_sem)
    mine.wait()
    for copy in hops:
        copy.wait()
    hops = []
    for k in range(1, across):
        to = lax.rem(col + k, across)
        part = got.at[pl.ds(base, rows)]
        hops.append(hop(rows - 1 + k, part, part, (row * across + to) * 2 + core))
        hops[-1].start()
    for copy in hops:
        copy.wait()
    part = got.at[pl.ds(count + core * half, half)]
    last = hop(0, part, part, (row * across + col) * 2 + 1 - core)
    last.start()
    last.wait()
    own.wait()
    wait_direct(direct, got, send_sem, recv_sem)


def chips_of(count):
    across = 4 if count % 8 == 0 else 1
    return across, count // (2 * across)


def by_core(values):
    across, rows = chips_of(values.shape[0])
    values = values.reshape(rows, across, 2, *values.shape[1:])
    return jnp.swapaxes(values, 0, 2)


def exchange_sems(count, across, rows):
    dma = pltpu.SemaphoreType.DMA
    return [dma, dma((count,)), dma((count,)), dma((across + rows,)), dma((across + rows,))]


def fetch(direct, extra):
    count, high, wide = direct.shape
    across, rows = chips_of(count)
    vmem = pl.BlockSpec(memory_space=pltpu.VMEM)
    buffer = lambda *dims: pltpu.VMEM((*dims, high, wide), direct.dtype)
    return pl.pallas_call(
        lambda *refs: fetch_kernel(across, rows, *refs),
        out_shape=jax.ShapeDtypeStruct((count + 1, high, wide), direct.dtype),
        in_specs=[vmem, vmem],
        out_specs=vmem,
        scratch_shapes=[
            buffer(across, rows), buffer(across, rows), buffer(across - 1, rows),
            buffer(rows), buffer(rows - 1), *exchange_sems(count, across, rows)],
        compiler_params=pltpu.CompilerParams(collective_id=1, has_side_effects=True),
        name="fetch",
    )(direct, extra)


def give_back(direct, extra):
    count, high, wide = direct.shape
    across, rows = chips_of(count)
    vmem = pl.BlockSpec(memory_space=pltpu.VMEM)
    return pl.pallas_call(
        lambda *refs: return_kernel(across, rows, *refs),
        out_shape=jax.ShapeDtypeStruct((2 * count, high, wide), direct.dtype),
        in_specs=[vmem, vmem],
        out_specs=vmem,
        scratch_shapes=exchange_sems(count, across, rows),
        compiler_params=pltpu.CompilerParams(collective_id=2, has_side_effects=True),
        name="give_back",
    )(direct, extra)


def adam_update(params, moment_one, moment_two, gradient):
    fresh_one = BETA_FIRST * moment_one + (1.0 - BETA_FIRST) * gradient
    fresh_two = BETA_SECOND * moment_two + (1.0 - BETA_SECOND) * gradient * gradient
    fresh_params = params - STEP_SIZE * fresh_one / (jnp.sqrt(fresh_two) + EPSILON)
    return (fresh_params, fresh_one, fresh_two)


def per_device(
    volume,
    first_moment,
    second_moment,
    probe,
    measured,
    scan_rows,
    scan_cols,
    owner_ids,
    block_ids,
    interp_weights,
):
    tile_index = lax.axis_index("tile")
    tile_count = lax.axis_size("tile")
    block_count = volume.shape[0]
    block_rows = volume.shape[2]
    slab_width = volume.shape[3]
    probe_size = probe.shape[1]
    margin = probe_size // 2
    requests = owner_ids.shape[2]
    row_blocks = interp_weights.shape[2]
    per_slice = slab_width // block_rows
    layers = row_blocks // per_slice
    capacity = 2
    group_owner = owner_ids[0]
    group_block = block_ids[0]
    request_slots = jnp.arange(requests, dtype=jnp.int32)
    earlier = request_slots[None, :] < request_slots[:, None]
    same_owner = group_owner[:, :, None] == group_owner[:, None, :]
    group_rank = jnp.sum(same_owner & earlier[None], axis=2)
    my_owner = lax.dynamic_index_in_dim(group_owner, tile_index, 0, keepdims=False)
    my_rank = lax.dynamic_index_in_dim(group_rank, tile_index, 0, keepdims=False)
    slot_ids = jnp.arange(capacity, dtype=jnp.int32)
    serving = (group_owner == tile_index)[:, None, :] & (
        group_rank[:, None, :] == slot_ids[None, :, None]
    )
    send_block = jnp.sum(jnp.where(serving, group_block[:, None, :], 0), axis=2)
    send_valid = jnp.any(serving, axis=2)
    blocks = volume.astype(jnp.bfloat16)
    weight = interp_weights[0, 0]
    complement = 1.0 - weight
    block_size = (2 * block_rows, slab_width)
    flat = blocks.reshape(block_count, *block_size)
    extra_out = jnp.where(
        by_core(send_valid[:, 1])[..., None, None], flat[by_core(send_block[:, 1])], 0
    ).astype(jnp.bfloat16)
    incoming = fetch(flat[send_block[:, 0]], extra_out)
    fetched = (
        incoming[jnp.where(my_rank == 0, my_owner, tile_count)]
        .astype(jnp.float32)
        .reshape(row_blocks, 2, 2, block_rows, slab_width)
    )
    obj_rows = (
        weight[:, None, None, None] * fetched[:, 0]
        + complement[:, None, None, None] * fetched[:, 1]
    )
    object_tile = obj_rows.reshape(layers, per_slice, 2, block_rows, slab_width).transpose(
        0, 2, 1, 3, 4
    )
    object_tile = object_tile.reshape(layers, 2, slab_width, slab_width).astype(jnp.bfloat16)
    padded = with_halo(object_tile, (("tile", 3),), margin).astype(jnp.float32)
    grad_padded = local_gradient(padded, probe, scan_rows[0, 0], scan_cols[0, 0], measured[0, 0])
    edges = grad_padded.astype(jnp.bfloat16)
    from_left = from_behind(edges[..., margin + slab_width :], "tile", 1).astype(jnp.float32)
    from_right = from_behind(edges[..., :margin], "tile", -1).astype(jnp.float32)
    interior = grad_padded[..., margin : margin + slab_width]
    middle = jnp.zeros((layers, 2, slab_width, slab_width - 2 * margin), jnp.float32)
    interior = interior + jnp.concatenate([from_left, middle, from_right], axis=3)
    grad_rows = interior.reshape(layers, 2, per_slice, block_rows, slab_width).transpose(
        0, 2, 1, 3, 4
    )
    grad_rows = grad_rows.reshape(row_blocks, 2, block_rows, slab_width)
    request_grads = jnp.stack(
        [weight[:, None, None, None] * grad_rows, complement[:, None, None, None] * grad_rows],
        axis=1,
    )
    request_grads = request_grads.reshape(requests, *block_size).astype(jnp.bfloat16)
    owner_range = jnp.arange(tile_count, dtype=jnp.int32)
    first_of = (my_owner[None, :] == owner_range[:, None]) & (my_rank[None, :] == 0)
    back_index = jnp.sum(jnp.where(first_of, request_slots[None, :], 0), axis=1)
    second = jnp.sum(jnp.where(my_rank == 1, request_slots, 0))
    arrived = give_back(
        request_grads[back_index],
        lax.dynamic_index_in_dim(request_grads, second, 0, keepdims=False),
    )
    selector = (
        send_block[:, :, None] == jnp.arange(block_count, dtype=jnp.int32)[None, None, :]
    ) & send_valid[:, :, None]
    selector = jnp.concatenate(
        [selector[:, 0], by_core(selector[:, 1]).reshape(tile_count, block_count)], axis=0
    ).astype(jnp.bfloat16)
    grad_volume = jnp.einsum(
        "nb,nhw->bhw", selector, arrived, preferred_element_type=jnp.float32
    )
    rows_total = block_count * 2 * block_rows
    angles = lax.axis_size("angle")
    partial_sums = grad_volume.reshape(angles, rows_total // angles, slab_width)
    parts = lax.all_to_all(partial_sums.astype(jnp.bfloat16), "angle", 0, 0, tiled=True)
    share = jnp.sum(parts.astype(jnp.float32), axis=0)
    spread = jnp.broadcast_to(share[None], (angles, *share.shape))
    gradient = lax.all_to_all(spread, "angle", 0, 0, tiled=True).reshape(volume.shape)
    return adam_update(volume, first_moment, second_moment, gradient)


def solution(mesh):
    in_specs = (
        P("tile", None, None, None),
        P("tile", None, None, None),
        P("tile", None, None, None),
        P(),
        P("angle", "tile", None, None, None),
        P("angle", "tile", None),
        P("angle", "tile", None),
        P("angle", None, None),
        P("angle", None, None),
        P("angle", "tile", None),
    )
    out_specs = (
        P("tile", None, None, None),
        P("tile", None, None, None),
        P("tile", None, None, None),
    )
    return jax.shard_map(
        per_device, mesh=mesh, in_specs=in_specs, out_specs=out_specs, check_vma=False
    )
```

```python
import math

import jax
import jax.numpy as jnp
import numpy as np
from jax import lax
from jax.experimental import pallas as pl
from jax.experimental.pallas import tpu as pltpu
from jax.sharding import PartitionSpec as P

FRESNEL = 0.35
SMOOTHING = 0.25
BETA_FIRST = 0.9
BETA_SECOND = 0.999
STEP_SIZE = 0.05
EPSILON = 1e-08


def with_halo(cells, sides, width):
    for axis, dim in sides:
        count = lax.axis_size(axis)
        ends = count - 1
        head = lax.slice_in_dim(cells, 0, width, axis=dim)
        tail = lax.slice_in_dim(cells, cells.shape[dim] - width, cells.shape[dim], axis=dim)
        cells = jnp.concatenate(
            [
                lax.ppermute(tail, axis, [(i, (i + 1) % count) for i in range(ends)]),
                cells,
                lax.ppermute(head, axis, [((i + 1) % count, i) for i in range(ends)]),
            ],
            axis=dim,
        )
    return cells


def from_behind(array, axis, by):
    length = lax.axis_size(axis)
    pairs = [(i, i + by) for i in range(length) if 0 <= i + by < length]
    return lax.ppermute(array, axis, pairs)


def block_form(table):
    real = np.concatenate([np.concatenate([table.real, table.imag], 1),
                           np.concatenate([-table.imag, table.real], 1)], 0)
    real = real.astype(np.float32)
    head = real.astype(jnp.bfloat16)
    rest = (real - head.astype(np.float32)).astype(jnp.bfloat16)
    return head, rest


def operator_tables(length):
    index = np.arange(length)
    table = np.exp(-2j * np.pi * (np.outer(index, index) % length) / length) / math.sqrt(length)
    signed = np.where(index < length // 2, index, index - length)
    phase = np.exp(-2j * np.pi * FRESNEL * signed * signed / length)
    step = (table.conj() * phase[None, :]) @ table
    out = []
    for operator in (table, step):
        out += [*block_form(operator), *block_form(operator.conj())]
    return np.stack(out)


def split_bf16(x):
    head = x.astype(jnp.bfloat16)
    return head, (x - head.astype(jnp.float32)).astype(jnp.bfloat16)


def mm(a, b):
    return jnp.dot(a, b, preferred_element_type=jnp.float32)


def wave_kernel(size, chunk, rows_ref, cols_ref, obj_ref, probe_ref, amp_ref, tab_ref, acc_ref):
    probes = amp_ref.shape[0]
    n = size

    def two_sided(real, imag, right, left):
        stacked = jnp.concatenate([jnp.concatenate([r, i], 1) for r, i in zip(real, imag)], 0)
        head, rest = split_bf16(stacked)
        half = mm(head, tab_ref[right]) + (mm(rest, tab_ref[right]) + mm(head, tab_ref[right + 1]))
        out_real, out_imag = [], []
        for k in range(0, len(real), 2):
            one = half[k * n : (k + 1) * n]
            two = half[(k + 1) * n : (k + 2) * n]
            pair = jnp.concatenate(
                [jnp.concatenate([one[:, :n], two[:, :n]], 1),
                 jnp.concatenate([one[:, n:], two[:, n:]], 1)], 0)
            head, rest = split_bf16(pair)
            full = mm(tab_ref[left], head) + (mm(tab_ref[left], rest) + mm(tab_ref[left + 1], head))
            out_real += [full[:n, :n], full[:n, n:]]
            out_imag += [full[n:, :n], full[n:, n:]]
        return out_real, out_imag

    acc_ref[...] = jnp.zeros_like(acc_ref)
    p_real = probe_ref[0]
    p_imag = probe_ref[1]

    def body(step, carry):
        first = step * chunk
        place, trans = [], []
        for k in range(chunk):
            row = rows_ref[0, first + k]
            col = cols_ref[0, first + k]
            base = pl.multiple_of(jnp.minimum(col // n, 1) * n, n)
            shift = col - base
            top = pl.multiple_of(jnp.minimum(row // 8, n // 8 - 1) * 8, 8)
            down = row - top
            place.append((top, down, base, shift))
            back = lax.rem(2 * n - shift, 2 * n)
            up = lax.rem(n + 8 - down, n + 8)
            window = []
            for c in range(4):
                wide = obj_ref[c, pl.ds(top, n + 8), pl.ds(base, 2 * n)]
                part = pltpu.roll(pltpu.roll(wide, back, 1)[:, :n], up, 0)[:n]
                window.append(part + 1.0 if c % 2 == 0 else part)
            trans.append(window)
        w_real = [p_real * t[0] - p_imag * t[1] for t in trans]
        w_imag = [p_real * t[1] + p_imag * t[0] for t in trans]
        u_real, u_imag = two_sided(w_real, w_imag, 4, 6)
        w_real = [r * t[2] - i * t[3] for r, i, t in zip(u_real, u_imag, trans)]
        w_imag = [r * t[3] + i * t[2] for r, i, t in zip(u_real, u_imag, trans)]
        f_real, f_imag = two_sided(w_real, w_imag, 0, 2)
        g_real, g_imag = [], []
        for k in range(chunk):
            r, i = f_real[k], f_imag[k]
            scale = 1.0 - amp_ref[first + k].astype(jnp.float32) * lax.rsqrt(r * r + i * i + SMOOTHING)
            g_real.append(r * scale)
            g_imag.append(i * scale)
        g_real, g_imag = two_sided(g_real, g_imag, 2, 0)
        d_real = [u * r + v * i for u, v, r, i in zip(u_real, u_imag, g_real, g_imag)]
        d_imag = [u * i - v * r for u, v, r, i in zip(u_real, u_imag, g_real, g_imag)]
        b_real = [t[2] * r + t[3] * i for t, r, i in zip(trans, g_real, g_imag)]
        b_imag = [t[2] * i - t[3] * r for t, r, i in zip(trans, g_real, g_imag)]
        b_real, b_imag = two_sided(b_real, b_imag, 6, 4)
        for k in range(chunk):
            r, i = b_real[k], b_imag[k]
            parts = (p_real * r + p_imag * i, p_real * i - p_imag * r, d_real[k], d_imag[k])
            top, down, base, shift = place[k]
            for c in range(4):
                tall = jnp.concatenate([parts[c], jnp.zeros((8, n), jnp.float32)], 0)
                tall = pltpu.roll(tall, down, 0)
                wide = jnp.concatenate([tall, jnp.zeros_like(tall)], 1)
                wide = pltpu.roll(wide, shift, 1)
                acc_ref[c, pl.ds(top, n + 8), pl.ds(base, 2 * n)] += wide
        return carry

    lax.fori_loop(0, probes // chunk, body, 0)


def local_gradient(padded, probe, rows_list, cols_list, amplitudes):
    layers, parts, high, wide = padded.shape
    size = probe.shape[-1]
    probes = amplitudes.shape[0]
    chunk = 4 if probes % 4 == 0 else 2
    tables = jnp.asarray(operator_tables(size))
    smem = pl.BlockSpec(memory_space=pltpu.SMEM)
    vmem = pl.BlockSpec(memory_space=pltpu.VMEM)
    out = pl.pallas_call(
        lambda *refs: wave_kernel(size, chunk, *refs),
        out_shape=jax.ShapeDtypeStruct((layers * parts, high, wide), jnp.float32),
        in_specs=[smem, smem, vmem, vmem, vmem, vmem],
        out_specs=vmem,
        name="waves",
    )(
        rows_list.reshape(1, -1),
        cols_list.reshape(1, -1),
        padded.reshape(layers * parts, high, wide),
        probe,
        amplitudes,
        tables,
    )
    return out.reshape(layers, parts, high, wide)


MESH = pl.DeviceIdType.MESH


def place(tile, across):
    return tile % 2, tile // 2 % across, tile // (2 * across)


def greet(axis):
    count = lax.axis_size(axis)
    me = lax.axis_index(axis)
    barrier = pltpu.get_barrier_semaphore()

    def signal(d, carry):
        pl.semaphore_signal(
            barrier, inc=1, device_id={axis: lax.rem(me + d, count)}, device_id_type=MESH
        )
        return carry

    lax.fori_loop(1, count, signal, 0)
    pl.semaphore_wait(barrier, count - 1)


def direct_copy(d, source, target, send_sem, recv_sem):
    count = lax.axis_size("tile")
    me = lax.axis_index("tile")
    peer = lax.rem(me + d, count)
    return pltpu.make_async_remote_copy(
        src_ref=source.at[peer],
        dst_ref=target.at[me],
        send_sem=send_sem.at[d],
        recv_sem=recv_sem.at[d],
        device_id={"tile": peer},
        device_id_type=MESH,
    )


def start_direct(source, target, own_sem, send_sem, recv_sem):
    me = lax.axis_index("tile")
    own = pltpu.make_async_copy(source.at[me], target.at[me], own_sem)
    own.start()

    def start(d, carry):
        direct_copy(d, source, target, send_sem, recv_sem).start()
        return carry

    lax.fori_loop(1, lax.axis_size("tile"), start, 0)
    return own


def wait_direct(source, target, send_sem, recv_sem):
    def wait(d, carry):
        direct_copy(d, source, target, send_sem, recv_sem).wait()
        return carry

    lax.fori_loop(1, lax.axis_size("tile"), wait, 0)


def fetch_kernel(across, rows, direct, extra, got, near, near_sum, run, run_sum, far,
                 own_sem, send_sem, recv_sem, hop_send, hop_recv):
    count = lax.axis_size("tile")
    core, col, row = place(lax.axis_index("tile"), across)

    def hop(k, source, target, tile):
        return pltpu.make_async_remote_copy(
            src_ref=source, dst_ref=target, send_sem=hop_send.at[k], recv_sem=hop_recv.at[k],
            device_id={"tile": tile}, device_id_type=MESH)

    greet("tile")
    first = hop(0, extra.at[1 - core], near, (row * across + col) * 2 + 1 - core)
    first.start()
    first.wait()
    near_sum[...] = extra[core] + near[...]
    hops = []
    for k in range(1, across):
        to = lax.rem(col + k, across)
        hops.append(hop(k, near_sum.at[to], run.at[k - 1], (row * across + to) * 2 + core))
        hops[-1].start()
    own = start_direct(direct, got, own_sem, send_sem, recv_sem)
    for copy in hops:
        copy.wait()
    total = near_sum[col]
    for k in range(across - 1):
        total = total + run[k]
    run_sum[...] = total
    hops = []
    for k in range(1, rows):
        to = lax.rem(row + k, rows)
        hops.append(hop(across - 1 + k, run_sum.at[to], far.at[k - 1], (to * across + col) * 2 + core))
        hops[-1].start()
    for copy in hops:
        copy.wait()
    total = run_sum[row]
    for k in range(rows - 1):
        total = total + far[k]
    got[count] = total
    own.wait()
    wait_direct(direct, got, send_sem, recv_sem)


def return_kernel(across, rows, direct, extra, got,
                  own_sem, send_sem, recv_sem, hop_send, hop_recv):
    count = lax.axis_size("tile")
    core, col, row = place(lax.axis_index("tile"), across)
    half = across * rows

    def hop(k, source, target, tile):
        return pltpu.make_async_remote_copy(
            src_ref=source, dst_ref=target, send_sem=hop_send.at[k], recv_sem=hop_recv.at[k],
            device_id={"tile": tile}, device_id_type=MESH)

    greet("tile")
    base = count + core * half + col * rows
    mine = pltpu.make_async_copy(extra, got.at[base + row], hop_send.at[across + rows - 1])
    mine.start()
    hops = []
    for k in range(1, rows):
        to = lax.rem(row + k, rows)
        hops.append(hop(k, extra, got.at[base + row], (to * across + col) * 2 + core))
        hops[-1].start()
    own = start_direct(direct, got, own_sem, send_sem, recv_sem)
    mine.wait()
    for copy in hops:
        copy.wait()
    hops = []
    for k in range(1, across):
        to = lax.rem(col + k, across)
        part = got.at[pl.ds(base, rows)]
        hops.append(hop(rows - 1 + k, part, part, (row * across + to) * 2 + core))
        hops[-1].start()
    for copy in hops:
        copy.wait()
    part = got.at[pl.ds(count + core * half, half)]
    last = hop(0, part, part, (row * across + col) * 2 + 1 - core)
    last.start()
    last.wait()
    own.wait()
    wait_direct(direct, got, send_sem, recv_sem)


def chips_of(count):
    across = 4 if count % 8 == 0 else 1
    return across, count // (2 * across)


def by_core(values):
    across, rows = chips_of(values.shape[0])
    values = values.reshape(rows, across, 2, *values.shape[1:])
    return jnp.swapaxes(values, 0, 2)


def exchange_sems(count, across, rows):
    dma = pltpu.SemaphoreType.DMA
    return [dma, dma((count,)), dma((count,)), dma((across + rows,)), dma((across + rows,))]


def fetch(direct, extra):
    count, high, wide = direct.shape
    across, rows = chips_of(count)
    vmem = pl.BlockSpec(memory_space=pltpu.VMEM)
    buffer = lambda *dims: pltpu.VMEM((*dims, high, wide), direct.dtype)
    return pl.pallas_call(
        lambda *refs: fetch_kernel(across, rows, *refs),
        out_shape=jax.ShapeDtypeStruct((count + 1, high, wide), direct.dtype),
        in_specs=[vmem, vmem],
        out_specs=vmem,
        scratch_shapes=[
            buffer(across, rows), buffer(across, rows), buffer(across - 1, rows),
            buffer(rows), buffer(rows - 1), *exchange_sems(count, across, rows)],
        compiler_params=pltpu.CompilerParams(collective_id=1, has_side_effects=True),
        name="fetch",
    )(direct, extra)


def give_back(direct, extra):
    count, high, wide = direct.shape
    across, rows = chips_of(count)
    vmem = pl.BlockSpec(memory_space=pltpu.VMEM)
    return pl.pallas_call(
        lambda *refs: return_kernel(across, rows, *refs),
        out_shape=jax.ShapeDtypeStruct((2 * count, high, wide), direct.dtype),
        in_specs=[vmem, vmem],
        out_specs=vmem,
        scratch_shapes=exchange_sems(count, across, rows),
        compiler_params=pltpu.CompilerParams(collective_id=2, has_side_effects=True),
        name="give_back",
    )(direct, extra)


def angle_kernel(parts, out, landed, partial, other,
                 in_send, in_recv, pair_send, pair_recv, right_send, right_recv, left_send, left_recv):
    ring = parts.shape[0]
    me = lax.axis_index("angle")
    spot, side = me // 2, me % 2

    def copy(source, target, send_sem, recv_sem, to, at):
        return pltpu.make_async_remote_copy(
            src_ref=source, dst_ref=target, send_sem=send_sem, recv_sem=recv_sem,
            device_id={"angle": to * 2 + at}, device_id_type=MESH)

    barrier = pltpu.get_barrier_semaphore()
    for k in range(1, ring):
        pl.semaphore_signal(barrier, inc=1, device_id={"angle": lax.rem(spot + k, ring) * 2 + side},
                            device_id_type=MESH)
    pl.semaphore_signal(barrier, inc=1, device_id={"angle": spot * 2 + 1 - side}, device_id_type=MESH)
    pl.semaphore_wait(barrier, ring)

    copies = []
    for k in range(1, ring):
        to = lax.rem(spot + k, ring)
        copies.append(copy(parts.at[to], landed.at[k - 1], in_send.at[k - 1], in_recv.at[k - 1], to, side))
        copies[-1].start()
    for c in copies:
        c.wait()
    total = parts[spot].astype(jnp.float32)
    for k in range(ring - 1):
        total = total + landed[k].astype(jnp.float32)
    partial[...] = total
    pair = copy(partial.at[1 - side], other, pair_send.at[0], pair_recv.at[0], spot, 1 - side)
    pair.start()
    pair.wait()
    out[spot, side] = partial[side] + other[...]

    pair = copy(out.at[spot, side], out.at[spot, side], pair_send.at[1], pair_recv.at[1], spot, 1 - side)
    pair.start()
    right, left = lax.rem(spot + 1, ring), lax.rem(spot + ring - 1, ring)
    far = ring // 2
    reach = ((far, ring - 1 - far), (ring - 1 - far, far))
    chunk = (side, 1 - side)

    def to_right(j, step):
        block = out.at[lax.rem(spot + ring - step, ring), chunk[j]]
        return copy(block, block, right_send.at[j, step], right_recv.at[j, step], right, side)

    def to_left(j, step):
        block = out.at[lax.rem(spot + step, ring), chunk[j]]
        return copy(block, block, left_send.at[j, step], left_recv.at[j, step], left, side)

    def from_left(j, step):
        block = out.at[lax.rem(spot + ring - step - 1, ring), chunk[j]]
        return copy(block, block, right_send.at[j, step], right_recv.at[j, step], right, side)

    def from_right(j, step):
        block = out.at[lax.rem(spot + step + 1, ring), chunk[j]]
        return copy(block, block, left_send.at[j, step], left_recv.at[j, step], left, side)

    sent = []
    for j in range(2):
        if j == 1:
            pair.wait_send()
            incoming = out.at[spot, 1 - side]
            copy(incoming, incoming, pair_send.at[1], pair_recv.at[1], spot, 1 - side).wait_recv()
        sent += [to_right(j, 0), to_left(j, 0)]
        sent[-2].start()
        sent[-1].start()
    for step in range(far):
        for j in range(2):
            if step < reach[j][0]:
                from_left(j, step).wait_recv()
                if step + 1 < reach[j][0]:
                    sent.append(to_right(j, step + 1))
                    sent[-1].start()
            if step < reach[j][1]:
                from_right(j, step).wait_recv()
                if step + 1 < reach[j][1]:
                    sent.append(to_left(j, step + 1))
                    sent[-1].start()
    for c in sent:
        c.wait_send()


def sum_over_angle(parts):
    angles, high, wide = parts.shape
    ring = angles // 2
    vmem = pl.BlockSpec(memory_space=pltpu.VMEM)
    dma = pltpu.SemaphoreType.DMA
    ring_sems = dma((2, ring))
    out = pl.pallas_call(
        angle_kernel,
        out_shape=jax.ShapeDtypeStruct((ring, 2, high, wide), jnp.float32),
        in_specs=[vmem],
        out_specs=vmem,
        scratch_shapes=[
            pltpu.VMEM((ring - 1, 2, high, wide), parts.dtype),
            pltpu.VMEM((2, high, wide), jnp.float32),
            pltpu.VMEM((high, wide), jnp.float32),
            dma((ring - 1,)), dma((ring - 1,)), dma((2,)), dma((2,)),
            ring_sems, ring_sems, ring_sems, ring_sems],
        compiler_params=pltpu.CompilerParams(collective_id=3, has_side_effects=True),
        name="angle_sum",
    )(parts.reshape(ring, 2, high, wide))
    return out.reshape(angles, high, wide)


def adam_update(params, moment_one, moment_two, gradient):
    fresh_one = BETA_FIRST * moment_one + (1.0 - BETA_FIRST) * gradient
    fresh_two = BETA_SECOND * moment_two + (1.0 - BETA_SECOND) * gradient * gradient
    fresh_params = params - STEP_SIZE * fresh_one / (jnp.sqrt(fresh_two) + EPSILON)
    return (fresh_params, fresh_one, fresh_two)


def per_device(
    volume,
    first_moment,
    second_moment,
    probe,
    measured,
    scan_rows,
    scan_cols,
    owner_ids,
    block_ids,
    interp_weights,
):
    tile_index = lax.axis_index("tile")
    tile_count = lax.axis_size("tile")
    block_count = volume.shape[0]
    block_rows = volume.shape[2]
    slab_width = volume.shape[3]
    probe_size = probe.shape[1]
    margin = probe_size // 2
    requests = owner_ids.shape[2]
    row_blocks = interp_weights.shape[2]
    per_slice = slab_width // block_rows
    layers = row_blocks // per_slice
    group_owner = owner_ids[0]
    group_block = block_ids[0]
    request_slots = jnp.arange(requests, dtype=jnp.int32)
    my_owner = lax.dynamic_index_in_dim(group_owner, tile_index, 0, keepdims=False)
    earlier = request_slots[None, :] < request_slots[:, None]
    my_rank = jnp.sum((my_owner[:, None] == my_owner[None, :]) & earlier, axis=1)
    mine = group_owner == tile_index
    first_slot = jnp.min(jnp.where(mine, request_slots, requests), axis=1)
    last_slot = jnp.max(jnp.where(mine, request_slots, -1), axis=1)
    slots = jnp.stack([first_slot, last_slot], axis=1)
    send_valid = jnp.stack([last_slot >= 0, last_slot > first_slot], axis=1)
    chosen = slots[:, :, None] == request_slots[None, None, :]
    send_block = jnp.sum(jnp.where(chosen, group_block[:, None, :], 0), axis=2)
    blocks = volume.astype(jnp.bfloat16)
    weight = interp_weights[0, 0]
    complement = 1.0 - weight
    block_size = (2 * block_rows, slab_width)
    flat = blocks.reshape(block_count, *block_size)
    extra_out = jnp.where(
        by_core(send_valid[:, 1])[..., None, None], flat[by_core(send_block[:, 1])], 0
    ).astype(jnp.bfloat16)
    incoming = fetch(flat[send_block[:, 0]], extra_out)
    fetched = (
        incoming[jnp.where(my_rank == 0, my_owner, tile_count)]
        .astype(jnp.float32)
        .reshape(row_blocks, 2, 2, block_rows, slab_width)
    )
    obj_rows = (
        weight[:, None, None, None] * fetched[:, 0]
        + complement[:, None, None, None] * fetched[:, 1]
    )
    object_tile = obj_rows.reshape(layers, per_slice, 2, block_rows, slab_width).transpose(
        0, 2, 1, 3, 4
    )
    object_tile = object_tile.reshape(layers, 2, slab_width, slab_width).astype(jnp.bfloat16)
    padded = with_halo(object_tile, (("tile", 3),), margin).astype(jnp.float32)
    grad_padded = local_gradient(padded, probe, scan_rows[0, 0], scan_cols[0, 0], measured[0, 0])
    edges = grad_padded.astype(jnp.bfloat16)
    from_left = from_behind(edges[..., margin + slab_width :], "tile", 1).astype(jnp.float32)
    from_right = from_behind(edges[..., :margin], "tile", -1).astype(jnp.float32)
    interior = grad_padded[..., margin : margin + slab_width]
    middle = jnp.zeros((layers, 2, slab_width, slab_width - 2 * margin), jnp.float32)
    interior = interior + jnp.concatenate([from_left, middle, from_right], axis=3)
    grad_rows = interior.reshape(layers, 2, per_slice, block_rows, slab_width).transpose(
        0, 2, 1, 3, 4
    )
    grad_rows = grad_rows.reshape(row_blocks, 2, block_rows, slab_width)
    request_grads = jnp.stack(
        [weight[:, None, None, None] * grad_rows, complement[:, None, None, None] * grad_rows],
        axis=1,
    )
    request_grads = request_grads.reshape(requests, *block_size).astype(jnp.bfloat16)
    owner_range = jnp.arange(tile_count, dtype=jnp.int32)
    first_of = (my_owner[None, :] == owner_range[:, None]) & (my_rank[None, :] == 0)
    back_index = jnp.sum(jnp.where(first_of, request_slots[None, :], 0), axis=1)
    second = jnp.sum(jnp.where(my_rank == 1, request_slots, 0))
    arrived = give_back(
        request_grads[back_index],
        lax.dynamic_index_in_dim(request_grads, second, 0, keepdims=False),
    )
    selector = (
        send_block[:, :, None] == jnp.arange(block_count, dtype=jnp.int32)[None, None, :]
    ) & send_valid[:, :, None]
    selector = jnp.concatenate(
        [selector[:, 0], by_core(selector[:, 1]).reshape(tile_count, block_count)], axis=0
    ).astype(jnp.bfloat16)
    grad_volume = jnp.einsum(
        "nb,nhw->bhw", selector, arrived, preferred_element_type=jnp.float32
    )
    rows_total = block_count * 2 * block_rows
    angles = lax.axis_size("angle")
    partial_sums = grad_volume.reshape(angles, rows_total // angles, slab_width)
    gradient = sum_over_angle(partial_sums.astype(jnp.bfloat16)).reshape(volume.shape)
    return adam_update(volume, first_moment, second_moment, gradient)


def solution(mesh):
    in_specs = (
        P("tile", None, None, None),
        P("tile", None, None, None),
        P("tile", None, None, None),
        P(),
        P("angle", "tile", None, None, None),
        P("angle", "tile", None),
        P("angle", "tile", None),
        P("angle", None, None),
        P("angle", None, None),
        P("angle", "tile", None),
    )
    out_specs = (
        P("tile", None, None, None),
        P("tile", None, None, None),
        P("tile", None, None, None),
    )
    return jax.shard_map(
        per_device, mesh=mesh, in_specs=in_specs, out_specs=out_specs, check_vma=False
    )
```

```python
import math

import jax
import jax.numpy as jnp
import numpy as np
from jax import lax
from jax.experimental import pallas as pl
from jax.experimental.pallas import tpu as pltpu
from jax.sharding import PartitionSpec as P

FRESNEL = 0.35
SMOOTHING = 0.25
BETA_FIRST = 0.9
BETA_SECOND = 0.999
STEP_SIZE = 0.05
EPSILON = 1e-08


def with_halo(cells, sides, width):
    for axis, dim in sides:
        count = lax.axis_size(axis)
        ends = count - 1
        head = lax.slice_in_dim(cells, 0, width, axis=dim)
        tail = lax.slice_in_dim(cells, cells.shape[dim] - width, cells.shape[dim], axis=dim)
        cells = jnp.concatenate(
            [
                lax.ppermute(tail, axis, [(i, (i + 1) % count) for i in range(ends)]),
                cells,
                lax.ppermute(head, axis, [((i + 1) % count, i) for i in range(ends)]),
            ],
            axis=dim,
        )
    return cells


def from_behind(array, axis, by):
    length = lax.axis_size(axis)
    pairs = [(i, i + by) for i in range(length) if 0 <= i + by < length]
    return lax.ppermute(array, axis, pairs)


def block_form(table):
    real = np.concatenate([np.concatenate([table.real, table.imag], 1),
                           np.concatenate([-table.imag, table.real], 1)], 0)
    real = real.astype(np.float32)
    head = real.astype(jnp.bfloat16)
    rest = (real - head.astype(np.float32)).astype(jnp.bfloat16)
    return head, rest


def operator_tables(length):
    index = np.arange(length)
    table = np.exp(-2j * np.pi * (np.outer(index, index) % length) / length) / math.sqrt(length)
    signed = np.where(index < length // 2, index, index - length)
    phase = np.exp(-2j * np.pi * FRESNEL * signed * signed / length)
    step = (table.conj() * phase[None, :]) @ table
    out = []
    for operator in (table, step):
        out += [*block_form(operator), *block_form(operator.conj())]
    return np.stack(out)


def split_bf16(x):
    head = x.astype(jnp.bfloat16)
    return head, (x - head.astype(jnp.float32)).astype(jnp.bfloat16)


def mm(a, b):
    return jnp.dot(a, b, preferred_element_type=jnp.float32)


def wave_kernel(size, chunk, rows_ref, cols_ref, obj_ref, probe_ref, amp_ref, tab_ref, acc_ref):
    probes = amp_ref.shape[0]
    n = size

    def two_sided(real, imag, right, left):
        stacked = jnp.concatenate([jnp.concatenate([r, i], 1) for r, i in zip(real, imag)], 0)
        head, rest = split_bf16(stacked)
        half = mm(head, tab_ref[right]) + (mm(rest, tab_ref[right]) + mm(head, tab_ref[right + 1]))
        out_real, out_imag = [], []
        for k in range(0, len(real), 2):
            one = half[k * n : (k + 1) * n]
            two = half[(k + 1) * n : (k + 2) * n]
            pair = jnp.concatenate(
                [jnp.concatenate([one[:, :n], two[:, :n]], 1),
                 jnp.concatenate([one[:, n:], two[:, n:]], 1)], 0)
            head, rest = split_bf16(pair)
            full = mm(tab_ref[left], head) + (mm(tab_ref[left], rest) + mm(tab_ref[left + 1], head))
            out_real += [full[:n, :n], full[:n, n:]]
            out_imag += [full[n:, :n], full[n:, n:]]
        return out_real, out_imag

    acc_ref[...] = jnp.zeros_like(acc_ref)
    p_real = probe_ref[0]
    p_imag = probe_ref[1]

    def body(step, carry):
        first = step * chunk
        place, trans = [], []
        for k in range(chunk):
            row = rows_ref[0, first + k]
            col = cols_ref[0, first + k]
            base = pl.multiple_of(jnp.minimum(col // n, 1) * n, n)
            shift = col - base
            top = pl.multiple_of(jnp.minimum(row // 8, n // 8 - 1) * 8, 8)
            down = row - top
            place.append((top, down, base, shift))
            back = lax.rem(2 * n - shift, 2 * n)
            up = lax.rem(n + 8 - down, n + 8)
            window = []
            for c in range(4):
                wide = obj_ref[c, pl.ds(top, n + 8), pl.ds(base, 2 * n)]
                part = pltpu.roll(pltpu.roll(wide, back, 1)[:, :n], up, 0)[:n]
                window.append(part + 1.0 if c % 2 == 0 else part)
            trans.append(window)
        w_real = [p_real * t[0] - p_imag * t[1] for t in trans]
        w_imag = [p_real * t[1] + p_imag * t[0] for t in trans]
        u_real, u_imag = two_sided(w_real, w_imag, 4, 6)
        w_real = [r * t[2] - i * t[3] for r, i, t in zip(u_real, u_imag, trans)]
        w_imag = [r * t[3] + i * t[2] for r, i, t in zip(u_real, u_imag, trans)]
        f_real, f_imag = two_sided(w_real, w_imag, 0, 2)
        g_real, g_imag = [], []
        for k in range(chunk):
            r, i = f_real[k], f_imag[k]
            scale = 1.0 - amp_ref[first + k].astype(jnp.float32) * lax.rsqrt(r * r + i * i + SMOOTHING)
            g_real.append(r * scale)
            g_imag.append(i * scale)
        g_real, g_imag = two_sided(g_real, g_imag, 2, 0)
        d_real = [u * r + v * i for u, v, r, i in zip(u_real, u_imag, g_real, g_imag)]
        d_imag = [u * i - v * r for u, v, r, i in zip(u_real, u_imag, g_real, g_imag)]
        b_real = [t[2] * r + t[3] * i for t, r, i in zip(trans, g_real, g_imag)]
        b_imag = [t[2] * i - t[3] * r for t, r, i in zip(trans, g_real, g_imag)]
        b_real, b_imag = two_sided(b_real, b_imag, 6, 4)
        for k in range(chunk):
            r, i = b_real[k], b_imag[k]
            parts = (p_real * r + p_imag * i, p_real * i - p_imag * r, d_real[k], d_imag[k])
            top, down, base, shift = place[k]
            for c in range(4):
                tall = jnp.concatenate([parts[c], jnp.zeros((8, n), jnp.float32)], 0)
                tall = pltpu.roll(tall, down, 0)
                wide = jnp.concatenate([tall, jnp.zeros_like(tall)], 1)
                wide = pltpu.roll(wide, shift, 1)
                acc_ref[c, pl.ds(top, n + 8), pl.ds(base, 2 * n)] += wide
        return carry

    lax.fori_loop(0, probes // chunk, body, 0)


def local_gradient(padded, probe, rows_list, cols_list, amplitudes):
    layers, parts, high, wide = padded.shape
    size = probe.shape[-1]
    probes = amplitudes.shape[0]
    chunk = 4 if probes % 4 == 0 else 2
    tables = jnp.asarray(operator_tables(size))
    smem = pl.BlockSpec(memory_space=pltpu.SMEM)
    vmem = pl.BlockSpec(memory_space=pltpu.VMEM)
    out = pl.pallas_call(
        lambda *refs: wave_kernel(size, chunk, *refs),
        out_shape=jax.ShapeDtypeStruct((layers * parts, high, wide), jnp.float32),
        in_specs=[smem, smem, vmem, vmem, vmem, vmem],
        out_specs=vmem,
        name="waves",
    )(
        rows_list.reshape(1, -1),
        cols_list.reshape(1, -1),
        padded.reshape(layers * parts, high, wide),
        probe,
        amplitudes,
        tables,
    )
    return out.reshape(layers, parts, high, wide)


MESH = pl.DeviceIdType.MESH


def place(tile, across):
    return tile % 2, tile // 2 % across, tile // (2 * across)


def greet(axis):
    count = lax.axis_size(axis)
    me = lax.axis_index(axis)
    barrier = pltpu.get_barrier_semaphore()

    def signal(d, carry):
        pl.semaphore_signal(
            barrier, inc=1, device_id={axis: lax.rem(me + d, count)}, device_id_type=MESH
        )
        return carry

    lax.fori_loop(1, count, signal, 0)
    pl.semaphore_wait(barrier, count - 1)


def direct_copy(d, source, target, send_sem, recv_sem):
    count = lax.axis_size("tile")
    me = lax.axis_index("tile")
    peer = lax.rem(me + d, count)
    return pltpu.make_async_remote_copy(
        src_ref=source.at[peer],
        dst_ref=target.at[me],
        send_sem=send_sem.at[d],
        recv_sem=recv_sem.at[d],
        device_id={"tile": peer},
        device_id_type=MESH,
    )


def start_direct(first, last, source, target, send_sem, recv_sem):
    def start(d, carry):
        direct_copy(d, source, target, send_sem, recv_sem).start()
        return carry

    lax.fori_loop(first, last, start, 0)


def keep_own(source, target, own_sem):
    me = lax.axis_index("tile")
    own = pltpu.make_async_copy(source.at[me], target.at[me], own_sem)
    own.start()
    return own


def wait_direct(source, target, send_sem, recv_sem):
    def wait(d, carry):
        direct_copy(d, source, target, send_sem, recv_sem).wait()
        return carry

    lax.fori_loop(1, lax.axis_size("tile"), wait, 0)


def fetch_kernel(across, rows, direct, extra, got, near, near_sum, run, run_sum, far,
                 own_sem, send_sem, recv_sem, hop_send, hop_recv):
    count = lax.axis_size("tile")
    core, col, row = place(lax.axis_index("tile"), across)

    def hop(k, source, target, tile):
        return pltpu.make_async_remote_copy(
            src_ref=source, dst_ref=target, send_sem=hop_send.at[k], recv_sem=hop_recv.at[k],
            device_id={"tile": tile}, device_id_type=MESH)

    greet("tile")
    first = hop(0, extra.at[1 - core], near, (row * across + col) * 2 + 1 - core)
    first.start()
    start_direct(1, count // 2, direct, got, send_sem, recv_sem)
    own = keep_own(direct, got, own_sem)
    first.wait()
    near_sum[...] = extra[core] + near[...]
    hops = []
    for k in range(1, across):
        to = lax.rem(col + k, across)
        hops.append(hop(k, near_sum.at[to], run.at[k - 1], (row * across + to) * 2 + core))
        hops[-1].start()
    start_direct(count // 2, count, direct, got, send_sem, recv_sem)
    for copy in hops:
        copy.wait()
    total = near_sum[col]
    for k in range(across - 1):
        total = total + run[k]
    run_sum[...] = total
    hops = []
    for k in range(1, rows):
        to = lax.rem(row + k, rows)
        hops.append(hop(across - 1 + k, run_sum.at[to], far.at[k - 1], (to * across + col) * 2 + core))
        hops[-1].start()
    for copy in hops:
        copy.wait()
    total = run_sum[row]
    for k in range(rows - 1):
        total = total + far[k]
    got[count] = total
    own.wait()
    wait_direct(direct, got, send_sem, recv_sem)


def return_kernel(across, rows, direct, extra, got,
                  own_sem, send_sem, recv_sem, hop_send, hop_recv):
    count = lax.axis_size("tile")
    core, col, row = place(lax.axis_index("tile"), across)
    half = across * rows

    def hop(k, source, target, tile):
        return pltpu.make_async_remote_copy(
            src_ref=source, dst_ref=target, send_sem=hop_send.at[k], recv_sem=hop_recv.at[k],
            device_id={"tile": tile}, device_id_type=MESH)

    greet("tile")
    base = count + core * half + col * rows
    mine = pltpu.make_async_copy(extra, got.at[base + row], hop_send.at[across + rows - 1])
    mine.start()
    hops = []
    for k in range(1, rows):
        to = lax.rem(row + k, rows)
        hops.append(hop(k, extra, got.at[base + row], (to * across + col) * 2 + core))
        hops[-1].start()
    start_direct(1, count // 2, direct, got, send_sem, recv_sem)
    own = keep_own(direct, got, own_sem)
    mine.wait()
    for copy in hops:
        copy.wait()
    hops = []
    for k in range(1, across):
        to = lax.rem(col + k, across)
        part = got.at[pl.ds(base, rows)]
        hops.append(hop(rows - 1 + k, part, part, (row * across + to) * 2 + core))
        hops[-1].start()
    start_direct(count // 2, count, direct, got, send_sem, recv_sem)
    for copy in hops:
        copy.wait()
    part = got.at[pl.ds(count + core * half, half)]
    last = hop(0, part, part, (row * across + col) * 2 + 1 - core)
    last.start()
    last.wait()
    own.wait()
    wait_direct(direct, got, send_sem, recv_sem)


def chips_of(count):
    across = 4 if count % 8 == 0 else 1
    return across, count // (2 * across)


def by_core(values):
    across, rows = chips_of(values.shape[0])
    values = values.reshape(rows, across, 2, *values.shape[1:])
    return jnp.swapaxes(values, 0, 2)


def exchange_sems(count, across, rows):
    dma = pltpu.SemaphoreType.DMA
    return [dma, dma((count,)), dma((count,)), dma((across + rows,)), dma((across + rows,))]


def fetch(direct, extra):
    count, high, wide = direct.shape
    across, rows = chips_of(count)
    vmem = pl.BlockSpec(memory_space=pltpu.VMEM)
    buffer = lambda *dims: pltpu.VMEM((*dims, high, wide), direct.dtype)
    return pl.pallas_call(
        lambda *refs: fetch_kernel(across, rows, *refs),
        out_shape=jax.ShapeDtypeStruct((count + 1, high, wide), direct.dtype),
        in_specs=[vmem, vmem],
        out_specs=vmem,
        scratch_shapes=[
            buffer(across, rows), buffer(across, rows), buffer(across - 1, rows),
            buffer(rows), buffer(rows - 1), *exchange_sems(count, across, rows)],
        compiler_params=pltpu.CompilerParams(collective_id=1, has_side_effects=True),
        name="fetch",
    )(direct, extra)


def give_back(direct, extra):
    count, high, wide = direct.shape
    across, rows = chips_of(count)
    vmem = pl.BlockSpec(memory_space=pltpu.VMEM)
    return pl.pallas_call(
        lambda *refs: return_kernel(across, rows, *refs),
        out_shape=jax.ShapeDtypeStruct((2 * count, high, wide), direct.dtype),
        in_specs=[vmem, vmem],
        out_specs=vmem,
        scratch_shapes=exchange_sems(count, across, rows),
        compiler_params=pltpu.CompilerParams(collective_id=2, has_side_effects=True),
        name="give_back",
    )(direct, extra)


def angle_kernel(parts, out, landed, partial, other,
                 in_send, in_recv, pair_send, pair_recv, right_send, right_recv, left_send, left_recv):
    ring = parts.shape[0]
    me = lax.axis_index("angle")
    spot, side = me // 2, me % 2

    def copy(source, target, send_sem, recv_sem, to, at):
        return pltpu.make_async_remote_copy(
            src_ref=source, dst_ref=target, send_sem=send_sem, recv_sem=recv_sem,
            device_id={"angle": to * 2 + at}, device_id_type=MESH)

    barrier = pltpu.get_barrier_semaphore()
    for k in range(1, ring):
        pl.semaphore_signal(barrier, inc=1, device_id={"angle": lax.rem(spot + k, ring) * 2 + side},
                            device_id_type=MESH)
    pl.semaphore_signal(barrier, inc=1, device_id={"angle": spot * 2 + 1 - side}, device_id_type=MESH)
    pl.semaphore_wait(barrier, ring)

    copies = []
    for k in range(1, ring):
        to = lax.rem(spot + k, ring)
        copies.append(copy(parts.at[to], landed.at[k - 1], in_send.at[k - 1], in_recv.at[k - 1], to, side))
        copies[-1].start()
    for c in copies:
        c.wait()
    total = parts[spot].astype(jnp.float32)
    for k in range(ring - 1):
        total = total + landed[k].astype(jnp.float32)
    partial[...] = total
    pair = copy(partial, other, pair_send, pair_recv, spot, 1 - side)
    pair.start()
    pair.wait()
    out[spot] = partial[...] + other[...]
    right, left = lax.rem(spot + 1, ring), lax.rem(spot + ring - 1, ring)
    far = ring // 2
    reach = ((far, ring - 1 - far), (ring - 1 - far, far))

    def to_right(j, step):
        block = out.at[lax.rem(spot + ring - step, ring), j]
        return copy(block, block, right_send.at[j, step], right_recv.at[j, step], right, side)

    def to_left(j, step):
        block = out.at[lax.rem(spot + step, ring), j]
        return copy(block, block, left_send.at[j, step], left_recv.at[j, step], left, side)

    def from_left(j, step):
        block = out.at[lax.rem(spot + ring - step - 1, ring), j]
        return copy(block, block, right_send.at[j, step], right_recv.at[j, step], right, side)

    def from_right(j, step):
        block = out.at[lax.rem(spot + step + 1, ring), j]
        return copy(block, block, left_send.at[j, step], left_recv.at[j, step], left, side)

    sent = []
    for j in range(2):
        sent += [to_right(j, 0), to_left(j, 0)]
        sent[-2].start()
        sent[-1].start()
    for step in range(far):
        for j in range(2):
            if step < reach[j][0]:
                from_left(j, step).wait_recv()
                if step + 1 < reach[j][0]:
                    sent.append(to_right(j, step + 1))
                    sent[-1].start()
            if step < reach[j][1]:
                from_right(j, step).wait_recv()
                if step + 1 < reach[j][1]:
                    sent.append(to_left(j, step + 1))
                    sent[-1].start()
    for c in sent:
        c.wait_send()


def sum_over_angle(parts):
    angles, high, wide = parts.shape
    ring = angles // 2
    vmem = pl.BlockSpec(memory_space=pltpu.VMEM)
    dma = pltpu.SemaphoreType.DMA
    ring_sems = dma((2, ring))
    out = pl.pallas_call(
        angle_kernel,
        out_shape=jax.ShapeDtypeStruct((ring, 2, high, wide), jnp.float32),
        in_specs=[vmem],
        out_specs=vmem,
        scratch_shapes=[
            pltpu.VMEM((ring - 1, 2, high, wide), parts.dtype),
            pltpu.VMEM((2, high, wide), jnp.float32),
            pltpu.VMEM((2, high, wide), jnp.float32),
            dma((ring - 1,)), dma((ring - 1,)), dma, dma,
            ring_sems, ring_sems, ring_sems, ring_sems],
        compiler_params=pltpu.CompilerParams(collective_id=3, has_side_effects=True),
        name="angle_sum",
    )(parts.reshape(ring, 2, high, wide))
    return out.reshape(angles, high, wide)


def adam_update(params, moment_one, moment_two, gradient):
    fresh_one = BETA_FIRST * moment_one + (1.0 - BETA_FIRST) * gradient
    fresh_two = BETA_SECOND * moment_two + (1.0 - BETA_SECOND) * gradient * gradient
    fresh_params = params - STEP_SIZE * fresh_one / (jnp.sqrt(fresh_two) + EPSILON)
    return (fresh_params, fresh_one, fresh_two)


def per_device(
    volume,
    first_moment,
    second_moment,
    probe,
    measured,
    scan_rows,
    scan_cols,
    owner_ids,
    block_ids,
    interp_weights,
):
    tile_index = lax.axis_index("tile")
    tile_count = lax.axis_size("tile")
    block_count = volume.shape[0]
    block_rows = volume.shape[2]
    slab_width = volume.shape[3]
    probe_size = probe.shape[1]
    margin = probe_size // 2
    requests = owner_ids.shape[2]
    row_blocks = interp_weights.shape[2]
    per_slice = slab_width // block_rows
    layers = row_blocks // per_slice
    group_owner = owner_ids[0]
    group_block = block_ids[0]
    request_slots = jnp.arange(requests, dtype=jnp.int32)
    my_owner = lax.dynamic_index_in_dim(group_owner, tile_index, 0, keepdims=False)
    earlier = request_slots[None, :] < request_slots[:, None]
    my_rank = jnp.sum((my_owner[:, None] == my_owner[None, :]) & earlier, axis=1)
    mine = group_owner == tile_index
    first_slot = jnp.min(jnp.where(mine, request_slots, requests), axis=1)
    last_slot = jnp.max(jnp.where(mine, request_slots, -1), axis=1)
    slots = jnp.stack([first_slot, last_slot], axis=1)
    send_valid = jnp.stack([last_slot >= 0, last_slot > first_slot], axis=1)
    chosen = slots[:, :, None] == request_slots[None, None, :]
    send_block = jnp.sum(jnp.where(chosen, group_block[:, None, :], 0), axis=2)
    blocks = volume.astype(jnp.bfloat16)
    weight = interp_weights[0, 0]
    complement = 1.0 - weight
    block_size = (2 * block_rows, slab_width)
    flat = blocks.reshape(block_count, *block_size)
    extra_out = jnp.where(
        by_core(send_valid[:, 1])[..., None, None], flat[by_core(send_block[:, 1])], 0
    ).astype(jnp.bfloat16)
    incoming = fetch(flat[send_block[:, 0]], extra_out)
    fetched = (
        incoming[jnp.where(my_rank == 0, my_owner, tile_count)]
        .astype(jnp.float32)
        .reshape(row_blocks, 2, 2, block_rows, slab_width)
    )
    obj_rows = (
        weight[:, None, None, None] * fetched[:, 0]
        + complement[:, None, None, None] * fetched[:, 1]
    )
    object_tile = obj_rows.reshape(layers, per_slice, 2, block_rows, slab_width).transpose(
        0, 2, 1, 3, 4
    )
    object_tile = object_tile.reshape(layers, 2, slab_width, slab_width).astype(jnp.bfloat16)
    padded = with_halo(object_tile, (("tile", 3),), margin).astype(jnp.float32)
    grad_padded = local_gradient(padded, probe, scan_rows[0, 0], scan_cols[0, 0], measured[0, 0])
    edges = grad_padded.astype(jnp.bfloat16)
    from_left = from_behind(edges[..., margin + slab_width :], "tile", 1).astype(jnp.float32)
    from_right = from_behind(edges[..., :margin], "tile", -1).astype(jnp.float32)
    interior = grad_padded[..., margin : margin + slab_width]
    middle = jnp.zeros((layers, 2, slab_width, slab_width - 2 * margin), jnp.float32)
    interior = interior + jnp.concatenate([from_left, middle, from_right], axis=3)
    grad_rows = interior.reshape(layers, 2, per_slice, block_rows, slab_width).transpose(
        0, 2, 1, 3, 4
    )
    grad_rows = grad_rows.reshape(row_blocks, 2, block_rows, slab_width)
    request_grads = jnp.stack(
        [weight[:, None, None, None] * grad_rows, complement[:, None, None, None] * grad_rows],
        axis=1,
    )
    request_grads = request_grads.reshape(requests, *block_size).astype(jnp.bfloat16)
    owner_range = jnp.arange(tile_count, dtype=jnp.int32)
    first_of = (my_owner[None, :] == owner_range[:, None]) & (my_rank[None, :] == 0)
    back_index = jnp.sum(jnp.where(first_of, request_slots[None, :], 0), axis=1)
    second = jnp.sum(jnp.where(my_rank == 1, request_slots, 0))
    arrived = give_back(
        request_grads[back_index],
        lax.dynamic_index_in_dim(request_grads, second, 0, keepdims=False),
    )
    selector = (
        send_block[:, :, None] == jnp.arange(block_count, dtype=jnp.int32)[None, None, :]
    ) & send_valid[:, :, None]
    selector = jnp.concatenate(
        [selector[:, 0], by_core(selector[:, 1]).reshape(tile_count, block_count)], axis=0
    ).astype(jnp.bfloat16)
    grad_volume = jnp.einsum(
        "nb,nhw->bhw", selector, arrived, preferred_element_type=jnp.float32
    )
    rows_total = block_count * 2 * block_rows
    angles = lax.axis_size("angle")
    partial_sums = grad_volume.reshape(angles, rows_total // angles, slab_width)
    gradient = sum_over_angle(partial_sums.astype(jnp.bfloat16)).reshape(volume.shape)
    return adam_update(volume, first_moment, second_moment, gradient)


def solution(mesh):
    in_specs = (
        P("tile", None, None, None),
        P("tile", None, None, None),
        P("tile", None, None, None),
        P(),
        P("angle", "tile", None, None, None),
        P("angle", "tile", None),
        P("angle", "tile", None),
        P("angle", None, None),
        P("angle", None, None),
        P("angle", "tile", None),
    )
    out_specs = (
        P("tile", None, None, None),
        P("tile", None, None, None),
        P("tile", None, None, None),
    )
    return jax.shard_map(
        per_device, mesh=mesh, in_specs=in_specs, out_specs=out_specs, check_vma=False
    )
```

```python
import math

import jax
import jax.numpy as jnp
import numpy as np
from jax import lax
from jax.experimental import pallas as pl
from jax.experimental.pallas import tpu as pltpu
from jax.sharding import PartitionSpec as P

FRESNEL = 0.35
SMOOTHING = 0.25
BETA_FIRST = 0.9
BETA_SECOND = 0.999
STEP_SIZE = 0.05
EPSILON = 1e-08


def from_behind(array, axis, by):
    length = lax.axis_size(axis)
    pairs = [(i, i + by) for i in range(length) if 0 <= i + by < length]
    return lax.ppermute(array, axis, pairs)


def block_form(table):
    real = np.concatenate([np.concatenate([table.real, table.imag], 1),
                           np.concatenate([-table.imag, table.real], 1)], 0)
    real = real.astype(np.float32)
    head = real.astype(jnp.bfloat16)
    rest = (real - head.astype(np.float32)).astype(jnp.bfloat16)
    return head, rest


def operator_tables(length):
    index = np.arange(length)
    table = np.exp(-2j * np.pi * (np.outer(index, index) % length) / length) / math.sqrt(length)
    signed = np.where(index < length // 2, index, index - length)
    phase = np.exp(-2j * np.pi * FRESNEL * signed * signed / length)
    step = (table.conj() * phase[None, :]) @ table
    out = []
    for operator in (table, step):
        out += [*block_form(operator), *block_form(operator.conj())]
    return np.stack(out)


def split_bf16(x):
    head = x.astype(jnp.bfloat16)
    return head, (x - head.astype(jnp.float32)).astype(jnp.bfloat16)


def mm(a, b):
    return jnp.dot(a, b, preferred_element_type=jnp.float32)


def wave_kernel(size, chunk, rows_ref, cols_ref, tile_ref, before_ref, after_ref,
                probe_ref, amp_ref, tab_ref, mid_ref, left_ref, right_ref, obj_ref, acc_ref):
    probes = amp_ref.shape[0]
    n = size

    def two_sided(real, imag, right, left):
        stacked = jnp.concatenate([jnp.concatenate([r, i], 1) for r, i in zip(real, imag)], 0)
        head, rest = split_bf16(stacked)
        half = mm(head, tab_ref[right]) + (mm(rest, tab_ref[right]) + mm(head, tab_ref[right + 1]))
        out_real, out_imag = [], []
        for k in range(0, len(real), 2):
            one = half[k * n : (k + 1) * n]
            two = half[(k + 1) * n : (k + 2) * n]
            pair = jnp.concatenate(
                [jnp.concatenate([one[:, :n], two[:, :n]], 1),
                 jnp.concatenate([one[:, n:], two[:, n:]], 1)], 0)
            head, rest = split_bf16(pair)
            full = mm(tab_ref[left], head) + (mm(tab_ref[left], rest) + mm(tab_ref[left + 1], head))
            out_real += [full[:n, :n], full[:n, n:]]
            out_imag += [full[n:, :n], full[n:, n:]]
        return out_real, out_imag

    margin = before_ref.shape[2]
    inner = tile_ref.shape[2]
    for c in range(4):
        obj_ref[c] = jnp.concatenate(
            [ref[c].astype(jnp.float32) for ref in (before_ref, tile_ref, after_ref)], 1)
    acc_ref[...] = jnp.zeros_like(acc_ref)
    p_real = probe_ref[0]
    p_imag = probe_ref[1]

    def body(step, carry):
        first = step * chunk
        place, trans = [], []
        for k in range(chunk):
            row = rows_ref[0, first + k]
            col = cols_ref[0, first + k]
            base = pl.multiple_of(jnp.minimum(col // n, 1) * n, n)
            shift = col - base
            top = pl.multiple_of(jnp.minimum(row // 8, n // 8 - 1) * 8, 8)
            down = row - top
            place.append((top, down, base, shift))
            back = lax.rem(2 * n - shift, 2 * n)
            up = lax.rem(n + 8 - down, n + 8)
            window = []
            for c in range(4):
                wide = obj_ref[c, pl.ds(top, n + 8), pl.ds(base, 2 * n)]
                part = pltpu.roll(pltpu.roll(wide, back, 1)[:, :n], up, 0)[:n]
                window.append(part + 1.0 if c % 2 == 0 else part)
            trans.append(window)
        w_real = [p_real * t[0] - p_imag * t[1] for t in trans]
        w_imag = [p_real * t[1] + p_imag * t[0] for t in trans]
        u_real, u_imag = two_sided(w_real, w_imag, 4, 6)
        w_real = [r * t[2] - i * t[3] for r, i, t in zip(u_real, u_imag, trans)]
        w_imag = [r * t[3] + i * t[2] for r, i, t in zip(u_real, u_imag, trans)]
        f_real, f_imag = two_sided(w_real, w_imag, 0, 2)
        g_real, g_imag = [], []
        for k in range(chunk):
            r, i = f_real[k], f_imag[k]
            scale = 1.0 - amp_ref[first + k].astype(jnp.float32) * lax.rsqrt(r * r + i * i + SMOOTHING)
            g_real.append(r * scale)
            g_imag.append(i * scale)
        g_real, g_imag = two_sided(g_real, g_imag, 2, 0)
        d_real = [u * r + v * i for u, v, r, i in zip(u_real, u_imag, g_real, g_imag)]
        d_imag = [u * i - v * r for u, v, r, i in zip(u_real, u_imag, g_real, g_imag)]
        b_real = [t[2] * r + t[3] * i for t, r, i in zip(trans, g_real, g_imag)]
        b_imag = [t[2] * i - t[3] * r for t, r, i in zip(trans, g_real, g_imag)]
        b_real, b_imag = two_sided(b_real, b_imag, 6, 4)
        for k in range(chunk):
            r, i = b_real[k], b_imag[k]
            parts = (p_real * r + p_imag * i, p_real * i - p_imag * r, d_real[k], d_imag[k])
            top, down, base, shift = place[k]
            for c in range(4):
                tall = jnp.concatenate([parts[c], jnp.zeros((8, n), jnp.float32)], 0)
                tall = pltpu.roll(tall, down, 0)
                wide = jnp.concatenate([tall, jnp.zeros_like(tall)], 1)
                wide = pltpu.roll(wide, shift, 1)
                acc_ref[c, pl.ds(top, n + 8), pl.ds(base, 2 * n)] += wide
        return carry

    lax.fori_loop(0, probes // chunk, body, 0)
    for c in range(4):
        total = acc_ref[c]
        mid_ref[c] = total[:, margin : margin + inner]
        left_ref[c] = total[:, :margin].astype(left_ref.dtype)
        right_ref[c] = total[:, margin + inner :].astype(right_ref.dtype)


def local_gradient(tile, before, after, probe, rows_list, cols_list, amplitudes):
    channels, high, inner = tile.shape
    margin = before.shape[2]
    size = probe.shape[-1]
    probes = amplitudes.shape[0]
    chunk = 4 if probes % 4 == 0 else 2
    tables = jnp.asarray(operator_tables(size))
    smem = pl.BlockSpec(memory_space=pltpu.SMEM)
    vmem = pl.BlockSpec(memory_space=pltpu.VMEM)
    padded = pltpu.VMEM((channels, high, inner + 2 * margin), jnp.float32)
    edge = jax.ShapeDtypeStruct(before.shape, jnp.bfloat16)
    return pl.pallas_call(
        lambda *refs: wave_kernel(size, chunk, *refs),
        out_shape=(jax.ShapeDtypeStruct(tile.shape, jnp.float32), edge, edge),
        in_specs=[smem, smem] + [vmem] * 6,
        out_specs=(vmem, vmem, vmem),
        scratch_shapes=[padded, padded],
        name="waves",
    )(rows_list.reshape(1, -1), cols_list.reshape(1, -1), tile, before, after, probe, amplitudes, tables)


MESH = pl.DeviceIdType.MESH


def place(tile, across):
    return tile % 2, tile // 2 % across, tile // (2 * across)


def greet(axis):
    count = lax.axis_size(axis)
    me = lax.axis_index(axis)
    barrier = pltpu.get_barrier_semaphore()

    def signal(d, carry):
        pl.semaphore_signal(
            barrier, inc=1, device_id={axis: lax.rem(me + d, count)}, device_id_type=MESH
        )
        return carry

    lax.fori_loop(1, count, signal, 0)
    pl.semaphore_wait(barrier, count - 1)


def direct_copy(d, source, target, send_sem, recv_sem):
    count = lax.axis_size("tile")
    me = lax.axis_index("tile")
    peer = lax.rem(me + d, count)
    return pltpu.make_async_remote_copy(
        src_ref=source.at[peer],
        dst_ref=target.at[me],
        send_sem=send_sem.at[d],
        recv_sem=recv_sem.at[d],
        device_id={"tile": peer},
        device_id_type=MESH,
    )


def start_direct(first, last, source, target, send_sem, recv_sem):
    def start(d, carry):
        direct_copy(d, source, target, send_sem, recv_sem).start()
        return carry

    lax.fori_loop(first, last, start, 0)


def keep_own(source, target, own_sem):
    me = lax.axis_index("tile")
    own = pltpu.make_async_copy(source.at[me], target.at[me], own_sem)
    own.start()
    return own


def wait_direct(source, target, send_sem, recv_sem):
    def wait(d, carry):
        direct_copy(d, source, target, send_sem, recv_sem).wait()
        return carry

    lax.fori_loop(1, lax.axis_size("tile"), wait, 0)


def fetch_kernel(across, rows, ids, second_ids, second_valid, blocks, got, direct, extra, near, near_sum, run, run_sum, far,
                 own_sem, send_sem, recv_sem, hop_send, hop_recv):
    count = lax.axis_size("tile")
    core, col, row = place(lax.axis_index("tile"), across)

    def hop(k, source, target, tile):
        return pltpu.make_async_remote_copy(
            src_ref=source, dst_ref=target, send_sem=hop_send.at[k], recv_sem=hop_recv.at[k],
            device_id={"tile": tile}, device_id_type=MESH)

    def fill_extra(e, carry):
        block = jnp.where(second_valid[0, e] > 0, blocks[second_ids[0, e]], 0.0)
        extra[e // (across * rows), e // rows % across, e % rows] = block.astype(extra.dtype)
        return carry

    def fill_direct(t, carry):
        direct[t] = blocks[ids[0, t]].astype(direct.dtype)
        return carry

    lax.fori_loop(0, count, fill_extra, 0)
    lax.fori_loop(0, count, fill_direct, 0)
    greet("tile")
    first = hop(0, extra.at[1 - core], near, (row * across + col) * 2 + 1 - core)
    first.start()
    start_direct(1, count // 2, direct, got, send_sem, recv_sem)
    own = keep_own(direct, got, own_sem)
    first.wait()
    near_sum[...] = extra[core] + near[...]
    hops = []
    for k in range(1, across):
        to = lax.rem(col + k, across)
        hops.append(hop(k, near_sum.at[to], run.at[k - 1], (row * across + to) * 2 + core))
        hops[-1].start()
    start_direct(count // 2, count, direct, got, send_sem, recv_sem)
    for copy in hops:
        copy.wait()
    total = near_sum[col]
    for k in range(across - 1):
        total = total + run[k]
    run_sum[...] = total
    hops = []
    for k in range(1, rows):
        to = lax.rem(row + k, rows)
        hops.append(hop(across - 1 + k, run_sum.at[to], far.at[k - 1], (to * across + col) * 2 + core))
        hops[-1].start()
    for copy in hops:
        copy.wait()
    total = run_sum[row]
    for k in range(rows - 1):
        total = total + far[k]
    got[count] = total
    own.wait()
    wait_direct(direct, got, send_sem, recv_sem)


def return_kernel(across, rows, direct, extra, got,
                  own_sem, send_sem, recv_sem, hop_send, hop_recv):
    count = lax.axis_size("tile")
    core, col, row = place(lax.axis_index("tile"), across)
    half = across * rows

    def hop(k, source, target, tile):
        return pltpu.make_async_remote_copy(
            src_ref=source, dst_ref=target, send_sem=hop_send.at[k], recv_sem=hop_recv.at[k],
            device_id={"tile": tile}, device_id_type=MESH)

    greet("tile")
    base = count + core * half + col * rows
    mine = pltpu.make_async_copy(extra, got.at[base + row], hop_send.at[across + rows - 1])
    mine.start()
    hops = []
    for k in range(1, rows):
        to = lax.rem(row + k, rows)
        hops.append(hop(k, extra, got.at[base + row], (to * across + col) * 2 + core))
        hops[-1].start()
    start_direct(1, count // 2, direct, got, send_sem, recv_sem)
    own = keep_own(direct, got, own_sem)
    mine.wait()
    for copy in hops:
        copy.wait()
    hops = []
    for k in range(1, across):
        to = lax.rem(col + k, across)
        part = got.at[pl.ds(base, rows)]
        hops.append(hop(rows - 1 + k, part, part, (row * across + to) * 2 + core))
        hops[-1].start()
    start_direct(count // 2, count, direct, got, send_sem, recv_sem)
    for copy in hops:
        copy.wait()
    part = got.at[pl.ds(count + core * half, half)]
    last = hop(0, part, part, (row * across + col) * 2 + 1 - core)
    last.start()
    last.wait()
    own.wait()
    wait_direct(direct, got, send_sem, recv_sem)


def chips_of(count):
    across = 4 if count % 8 == 0 else 1
    return across, count // (2 * across)


def by_core(values):
    across, rows = chips_of(values.shape[0])
    values = values.reshape(rows, across, 2, *values.shape[1:])
    return jnp.swapaxes(values, 0, 2)


def exchange_sems(count, across, rows):
    dma = pltpu.SemaphoreType.DMA
    return [dma, dma((count,)), dma((count,)), dma((across + rows,)), dma((across + rows,))]


def fetch(blocks, ids, second_ids, second_valid):
    high, wide = blocks.shape[1:]
    count = ids.shape[0]
    scalars = [x.reshape(1, count).astype(jnp.int32) for x in (ids, second_ids, second_valid)]
    across, rows = chips_of(count)
    smem = pl.BlockSpec(memory_space=pltpu.SMEM)
    vmem = pl.BlockSpec(memory_space=pltpu.VMEM)
    buffer = lambda *dims: pltpu.VMEM((*dims, high, wide), jnp.bfloat16)
    return pl.pallas_call(
        lambda *refs: fetch_kernel(across, rows, *refs),
        out_shape=jax.ShapeDtypeStruct((count + 1, high, wide), jnp.bfloat16),
        in_specs=[smem, smem, smem, vmem],
        out_specs=vmem,
        scratch_shapes=[
            buffer(count), buffer(2, across, rows),
            buffer(across, rows), buffer(across, rows), buffer(across - 1, rows),
            buffer(rows), buffer(rows - 1), *exchange_sems(count, across, rows)],
        compiler_params=pltpu.CompilerParams(collective_id=1, has_side_effects=True),
        name="fetch",
    )(*scalars, blocks)


def give_back(direct, extra):
    count, high, wide = direct.shape
    across, rows = chips_of(count)
    vmem = pl.BlockSpec(memory_space=pltpu.VMEM)
    return pl.pallas_call(
        lambda *refs: return_kernel(across, rows, *refs),
        out_shape=jax.ShapeDtypeStruct((2 * count, high, wide), direct.dtype),
        in_specs=[vmem, vmem],
        out_specs=vmem,
        scratch_shapes=exchange_sems(count, across, rows),
        compiler_params=pltpu.CompilerParams(collective_id=2, has_side_effects=True),
        name="give_back",
    )(direct, extra)


def angle_kernel(parts, out, landed, partial, other,
                 in_send, in_recv, pair_send, pair_recv, right_send, right_recv, left_send, left_recv):
    ring = parts.shape[0]
    me = lax.axis_index("angle")
    spot, side = me // 2, me % 2

    def copy(source, target, send_sem, recv_sem, to, at):
        return pltpu.make_async_remote_copy(
            src_ref=source, dst_ref=target, send_sem=send_sem, recv_sem=recv_sem,
            device_id={"angle": to * 2 + at}, device_id_type=MESH)

    barrier = pltpu.get_barrier_semaphore()
    for k in range(1, ring):
        pl.semaphore_signal(barrier, inc=1, device_id={"angle": lax.rem(spot + k, ring) * 2 + side},
                            device_id_type=MESH)
    pl.semaphore_signal(barrier, inc=1, device_id={"angle": spot * 2 + 1 - side}, device_id_type=MESH)
    pl.semaphore_wait(barrier, ring)

    copies = []
    for k in range(1, ring):
        to = lax.rem(spot + k, ring)
        copies.append(copy(parts.at[to], landed.at[k - 1], in_send.at[k - 1], in_recv.at[k - 1], to, side))
        copies[-1].start()
    for c in copies:
        c.wait()
    total = parts[spot].astype(jnp.float32)
    for k in range(ring - 1):
        total = total + landed[k].astype(jnp.float32)
    partial[...] = total
    pair = copy(partial, other, pair_send, pair_recv, spot, 1 - side)
    pair.start()
    pair.wait()
    out[spot] = partial[...] + other[...]
    right, left = lax.rem(spot + 1, ring), lax.rem(spot + ring - 1, ring)
    far = ring // 2
    reach = ((far, ring - 1 - far), (ring - 1 - far, far))

    def to_right(j, step):
        block = out.at[lax.rem(spot + ring - step, ring), j]
        return copy(block, block, right_send.at[j, step], right_recv.at[j, step], right, side)

    def to_left(j, step):
        block = out.at[lax.rem(spot + step, ring), j]
        return copy(block, block, left_send.at[j, step], left_recv.at[j, step], left, side)

    def from_left(j, step):
        block = out.at[lax.rem(spot + ring - step - 1, ring), j]
        return copy(block, block, right_send.at[j, step], right_recv.at[j, step], right, side)

    def from_right(j, step):
        block = out.at[lax.rem(spot + step + 1, ring), j]
        return copy(block, block, left_send.at[j, step], left_recv.at[j, step], left, side)

    sent = []
    for j in range(2):
        sent += [to_right(j, 0), to_left(j, 0)]
        sent[-2].start()
        sent[-1].start()
    for step in range(far):
        for j in range(2):
            if step < reach[j][0]:
                from_left(j, step).wait_recv()
                if step + 1 < reach[j][0]:
                    sent.append(to_right(j, step + 1))
                    sent[-1].start()
            if step < reach[j][1]:
                from_right(j, step).wait_recv()
                if step + 1 < reach[j][1]:
                    sent.append(to_left(j, step + 1))
                    sent[-1].start()
    for c in sent:
        c.wait_send()


def sum_over_angle(parts):
    angles, high, wide = parts.shape
    ring = angles // 2
    vmem = pl.BlockSpec(memory_space=pltpu.VMEM)
    dma = pltpu.SemaphoreType.DMA
    ring_sems = dma((2, ring))
    out = pl.pallas_call(
        angle_kernel,
        out_shape=jax.ShapeDtypeStruct((ring, 2, high, wide), jnp.float32),
        in_specs=[vmem],
        out_specs=vmem,
        scratch_shapes=[
            pltpu.VMEM((ring - 1, 2, high, wide), parts.dtype),
            pltpu.VMEM((2, high, wide), jnp.float32),
            pltpu.VMEM((2, high, wide), jnp.float32),
            dma((ring - 1,)), dma((ring - 1,)), dma, dma,
            ring_sems, ring_sems, ring_sems, ring_sems],
        compiler_params=pltpu.CompilerParams(collective_id=3, has_side_effects=True),
        name="angle_sum",
    )(parts.reshape(ring, 2, high, wide))
    return out.reshape(angles, high, wide)


def adam_update(params, moment_one, moment_two, gradient):
    fresh_one = BETA_FIRST * moment_one + (1.0 - BETA_FIRST) * gradient
    fresh_two = BETA_SECOND * moment_two + (1.0 - BETA_SECOND) * gradient * gradient
    fresh_params = params - STEP_SIZE * fresh_one / (jnp.sqrt(fresh_two) + EPSILON)
    return (fresh_params, fresh_one, fresh_two)


def per_device(
    volume,
    first_moment,
    second_moment,
    probe,
    measured,
    scan_rows,
    scan_cols,
    owner_ids,
    block_ids,
    interp_weights,
):
    tile_index = lax.axis_index("tile")
    tile_count = lax.axis_size("tile")
    block_count = volume.shape[0]
    block_rows = volume.shape[2]
    slab_width = volume.shape[3]
    probe_size = probe.shape[1]
    margin = probe_size // 2
    requests = owner_ids.shape[2]
    row_blocks = interp_weights.shape[2]
    per_slice = slab_width // block_rows
    layers = row_blocks // per_slice
    group_owner = owner_ids[0]
    group_block = block_ids[0]
    request_slots = jnp.arange(requests, dtype=jnp.int32)
    my_owner = lax.dynamic_index_in_dim(group_owner, tile_index, 0, keepdims=False)
    earlier = request_slots[None, :] < request_slots[:, None]
    my_rank = jnp.sum((my_owner[:, None] == my_owner[None, :]) & earlier, axis=1)
    mine = group_owner == tile_index
    first_slot = jnp.min(jnp.where(mine, request_slots, requests), axis=1)
    last_slot = jnp.max(jnp.where(mine, request_slots, -1), axis=1)
    slots = jnp.stack([first_slot, last_slot], axis=1)
    send_valid = jnp.stack([last_slot >= 0, last_slot > first_slot], axis=1)
    chosen = slots[:, :, None] == request_slots[None, None, :]
    send_block = jnp.sum(jnp.where(chosen, group_block[:, None, :], 0), axis=2)
    weight = interp_weights[0, 0]
    complement = 1.0 - weight
    block_size = (2 * block_rows, slab_width)
    incoming = fetch(
        volume.reshape(block_count, *block_size),
        send_block[:, 0],
        by_core(send_block[:, 1]),
        by_core(send_valid[:, 1]),
    )
    fetched = (
        incoming[jnp.where(my_rank == 0, my_owner, tile_count)]
        .astype(jnp.float32)
        .reshape(row_blocks, 2, 2, block_rows, slab_width)
    )
    obj_rows = (
        weight[:, None, None, None] * fetched[:, 0]
        + complement[:, None, None, None] * fetched[:, 1]
    )
    object_tile = obj_rows.reshape(layers, per_slice, 2, block_rows, slab_width).transpose(
        0, 2, 1, 3, 4
    )
    object_tile = object_tile.reshape(layers, 2, slab_width, slab_width).astype(jnp.bfloat16)
    object_tile = object_tile.reshape(layers * 2, slab_width, slab_width)
    before = from_behind(object_tile[..., slab_width - margin :], "tile", 1)
    after = from_behind(object_tile[..., :margin], "tile", -1)
    interior, low_edge, high_edge = local_gradient(
        object_tile, before, after, probe, scan_rows[0, 0], scan_cols[0, 0], measured[0, 0]
    )
    from_left = from_behind(high_edge, "tile", 1).astype(jnp.float32)
    from_right = from_behind(low_edge, "tile", -1).astype(jnp.float32)
    middle = jnp.zeros((layers * 2, slab_width, slab_width - 2 * margin), jnp.float32)
    interior = interior + jnp.concatenate([from_left, middle, from_right], axis=2)
    grad_rows = interior.reshape(layers, 2, per_slice, block_rows, slab_width).transpose(
        0, 2, 1, 3, 4
    )
    grad_rows = grad_rows.reshape(row_blocks, 2, block_rows, slab_width)
    request_grads = jnp.stack(
        [weight[:, None, None, None] * grad_rows, complement[:, None, None, None] * grad_rows],
        axis=1,
    )
    request_grads = request_grads.reshape(requests, *block_size).astype(jnp.bfloat16)
    owner_range = jnp.arange(tile_count, dtype=jnp.int32)
    first_of = (my_owner[None, :] == owner_range[:, None]) & (my_rank[None, :] == 0)
    back_index = jnp.sum(jnp.where(first_of, request_slots[None, :], 0), axis=1)
    second = jnp.sum(jnp.where(my_rank == 1, request_slots, 0))
    arrived = give_back(
        request_grads[back_index],
        lax.dynamic_index_in_dim(request_grads, second, 0, keepdims=False),
    )
    selector = (
        send_block[:, :, None] == jnp.arange(block_count, dtype=jnp.int32)[None, None, :]
    ) & send_valid[:, :, None]
    selector = jnp.concatenate(
        [selector[:, 0], by_core(selector[:, 1]).reshape(tile_count, block_count)], axis=0
    ).astype(jnp.bfloat16)
    grad_volume = jnp.einsum(
        "nb,nhw->bhw", selector, arrived, preferred_element_type=jnp.float32
    )
    rows_total = block_count * 2 * block_rows
    angles = lax.axis_size("angle")
    partial_sums = grad_volume.reshape(angles, rows_total // angles, slab_width)
    gradient = sum_over_angle(partial_sums.astype(jnp.bfloat16)).reshape(volume.shape)
    return adam_update(volume, first_moment, second_moment, gradient)


def solution(mesh):
    in_specs = (
        P("tile", None, None, None),
        P("tile", None, None, None),
        P("tile", None, None, None),
        P(),
        P("angle", "tile", None, None, None),
        P("angle", "tile", None),
        P("angle", "tile", None),
        P("angle", None, None),
        P("angle", None, None),
        P("angle", "tile", None),
    )
    out_specs = (
        P("tile", None, None, None),
        P("tile", None, None, None),
        P("tile", None, None, None),
    )
    return jax.shard_map(
        per_device, mesh=mesh, in_specs=in_specs, out_specs=out_specs, check_vma=False
    )
```

```python
import math

import jax
import jax.numpy as jnp
import numpy as np
from jax import lax
from jax.experimental import pallas as pl
from jax.experimental.pallas import tpu as pltpu
from jax.sharding import PartitionSpec as P

FRESNEL = 0.35
SMOOTHING = 0.25
BETA_FIRST = 0.9
BETA_SECOND = 0.999
STEP_SIZE = 0.05
EPSILON = 1e-08


def from_behind(array, axis, by):
    length = lax.axis_size(axis)
    pairs = [(i, i + by) for i in range(length) if 0 <= i + by < length]
    return lax.ppermute(array, axis, pairs)


def block_form(table):
    real = np.concatenate([np.concatenate([table.real, table.imag], 1),
                           np.concatenate([-table.imag, table.real], 1)], 0)
    real = real.astype(np.float32)
    head = real.astype(jnp.bfloat16)
    rest = (real - head.astype(np.float32)).astype(jnp.bfloat16)
    return head, rest


def operator_tables(length):
    index = np.arange(length)
    table = np.exp(-2j * np.pi * (np.outer(index, index) % length) / length) / math.sqrt(length)
    signed = np.where(index < length // 2, index, index - length)
    phase = np.exp(-2j * np.pi * FRESNEL * signed * signed / length)
    step = (table.conj() * phase[None, :]) @ table
    out = []
    for operator in (table, step):
        out += [*block_form(operator), *block_form(operator.conj())]
    return np.stack(out)


def split_bf16(x):
    head = x.astype(jnp.bfloat16)
    return head, (x - head.astype(jnp.float32)).astype(jnp.bfloat16)


def mm(a, b):
    return jnp.dot(a, b, preferred_element_type=jnp.float32)


def wave_kernel(size, chunk, rows_ref, cols_ref, tile_ref, before_ref, after_ref,
                probe_ref, amp_ref, tab_ref, mid_ref, left_ref, right_ref, obj_ref, acc_ref):
    probes = amp_ref.shape[0]
    n = size

    def two_sided(real, imag, right, left):
        stacked = jnp.concatenate([jnp.concatenate([r, i], 1) for r, i in zip(real, imag)], 0)
        head, rest = split_bf16(stacked)
        half = mm(head, tab_ref[right]) + (mm(rest, tab_ref[right]) + mm(head, tab_ref[right + 1]))
        out_real, out_imag = [], []
        for k in range(0, len(real), 2):
            one = half[k * n : (k + 1) * n]
            two = half[(k + 1) * n : (k + 2) * n]
            pair = jnp.concatenate(
                [jnp.concatenate([one[:, :n], two[:, :n]], 1),
                 jnp.concatenate([one[:, n:], two[:, n:]], 1)], 0)
            head, rest = split_bf16(pair)
            full = mm(tab_ref[left], head) + (mm(tab_ref[left], rest) + mm(tab_ref[left + 1], head))
            out_real += [full[:n, :n], full[:n, n:]]
            out_imag += [full[n:, :n], full[n:, n:]]
        return out_real, out_imag

    margin = before_ref.shape[2]
    inner = tile_ref.shape[2]
    for c in range(4):
        obj_ref[c] = jnp.concatenate(
            [ref[c].astype(jnp.float32) for ref in (before_ref, tile_ref, after_ref)], 1)
    acc_ref[...] = jnp.zeros_like(acc_ref)
    p_real = probe_ref[0]
    p_imag = probe_ref[1]

    def body(step, carry):
        first = step * chunk
        place, trans = [], []
        for k in range(chunk):
            row = rows_ref[0, first + k]
            col = cols_ref[0, first + k]
            base = pl.multiple_of(jnp.minimum(col // n, 1) * n, n)
            shift = col - base
            top = pl.multiple_of(jnp.minimum(row // 8, n // 8 - 1) * 8, 8)
            down = row - top
            place.append((top, down, base, shift))
            back = lax.rem(2 * n - shift, 2 * n)
            up = lax.rem(n + 8 - down, n + 8)
            window = []
            for c in range(4):
                wide = obj_ref[c, pl.ds(top, n + 8), pl.ds(base, 2 * n)]
                part = pltpu.roll(pltpu.roll(wide, back, 1)[:, :n], up, 0)[:n]
                window.append(part + 1.0 if c % 2 == 0 else part)
            trans.append(window)
        w_real = [p_real * t[0] - p_imag * t[1] for t in trans]
        w_imag = [p_real * t[1] + p_imag * t[0] for t in trans]
        u_real, u_imag = two_sided(w_real, w_imag, 4, 6)
        w_real = [r * t[2] - i * t[3] for r, i, t in zip(u_real, u_imag, trans)]
        w_imag = [r * t[3] + i * t[2] for r, i, t in zip(u_real, u_imag, trans)]
        f_real, f_imag = two_sided(w_real, w_imag, 0, 2)
        g_real, g_imag = [], []
        for k in range(chunk):
            r, i = f_real[k], f_imag[k]
            scale = 1.0 - amp_ref[first + k].astype(jnp.float32) * lax.rsqrt(r * r + i * i + SMOOTHING)
            g_real.append(r * scale)
            g_imag.append(i * scale)
        g_real, g_imag = two_sided(g_real, g_imag, 2, 0)
        d_real = [u * r + v * i for u, v, r, i in zip(u_real, u_imag, g_real, g_imag)]
        d_imag = [u * i - v * r for u, v, r, i in zip(u_real, u_imag, g_real, g_imag)]
        b_real = [t[2] * r + t[3] * i for t, r, i in zip(trans, g_real, g_imag)]
        b_imag = [t[2] * i - t[3] * r for t, r, i in zip(trans, g_real, g_imag)]
        b_real, b_imag = two_sided(b_real, b_imag, 6, 4)
        for k in range(chunk):
            r, i = b_real[k], b_imag[k]
            parts = (p_real * r + p_imag * i, p_real * i - p_imag * r, d_real[k], d_imag[k])
            top, down, base, shift = place[k]
            for c in range(4):
                tall = jnp.concatenate([parts[c], jnp.zeros((8, n), jnp.float32)], 0)
                tall = pltpu.roll(tall, down, 0)
                wide = jnp.concatenate([tall, jnp.zeros_like(tall)], 1)
                wide = pltpu.roll(wide, shift, 1)
                acc_ref[c, pl.ds(top, n + 8), pl.ds(base, 2 * n)] += wide
        return carry

    lax.fori_loop(0, probes // chunk, body, 0)
    for c in range(4):
        total = acc_ref[c]
        mid_ref[c] = total[:, margin : margin + inner]
        left_ref[c] = total[:, :margin].astype(left_ref.dtype)
        right_ref[c] = total[:, margin + inner :].astype(right_ref.dtype)


def local_gradient(tile, before, after, probe, rows_list, cols_list, amplitudes):
    channels, high, inner = tile.shape
    margin = before.shape[2]
    size = probe.shape[-1]
    probes = amplitudes.shape[0]
    chunk = 4 if probes % 4 == 0 else 2
    tables = jnp.asarray(operator_tables(size))
    smem = pl.BlockSpec(memory_space=pltpu.SMEM)
    vmem = pl.BlockSpec(memory_space=pltpu.VMEM)
    padded = pltpu.VMEM((channels, high, inner + 2 * margin), jnp.float32)
    edge = jax.ShapeDtypeStruct(before.shape, jnp.bfloat16)
    return pl.pallas_call(
        lambda *refs: wave_kernel(size, chunk, *refs),
        out_shape=(jax.ShapeDtypeStruct(tile.shape, jnp.float32), edge, edge),
        in_specs=[smem, smem] + [vmem] * 6,
        out_specs=(vmem, vmem, vmem),
        scratch_shapes=[padded, padded],
        name="waves",
    )(rows_list.reshape(1, -1), cols_list.reshape(1, -1), tile, before, after, probe, amplitudes, tables)


MESH = pl.DeviceIdType.MESH


def place(tile, across):
    return tile % 2, tile // 2 % across, tile // (2 * across)


def greet(axis):
    count = lax.axis_size(axis)
    me = lax.axis_index(axis)
    barrier = pltpu.get_barrier_semaphore()

    def signal(d, carry):
        pl.semaphore_signal(
            barrier, inc=1, device_id={axis: lax.rem(me + d, count)}, device_id_type=MESH
        )
        return carry

    lax.fori_loop(1, count, signal, 0)
    pl.semaphore_wait(barrier, count - 1)


def direct_copy(d, source, target, send_sem, recv_sem):
    count = lax.axis_size("tile")
    me = lax.axis_index("tile")
    peer = lax.rem(me + d, count)
    return pltpu.make_async_remote_copy(
        src_ref=source.at[peer],
        dst_ref=target.at[me],
        send_sem=send_sem.at[d],
        recv_sem=recv_sem.at[d],
        device_id={"tile": peer},
        device_id_type=MESH,
    )


def start_direct(first, last, source, target, send_sem, recv_sem):
    count = lax.axis_size("tile")
    skip = 2 * chips_of(count)[0] - 1

    def start(k, carry):
        d = lax.rem(k - 1 + skip, count - 1) + 1
        direct_copy(d, source, target, send_sem, recv_sem).start()
        return carry

    lax.fori_loop(first, last, start, 0)


def keep_own(source, target, own_sem):
    me = lax.axis_index("tile")
    own = pltpu.make_async_copy(source.at[me], target.at[me], own_sem)
    own.start()
    return own


def wait_direct(source, target, send_sem, recv_sem):
    def wait(d, carry):
        direct_copy(d, source, target, send_sem, recv_sem).wait()
        return carry

    lax.fori_loop(1, lax.axis_size("tile"), wait, 0)


def fetch_kernel(across, rows, ids, second_ids, second_valid, blocks, got, direct, extra, near, near_sum, run, run_sum, far,
                 own_sem, send_sem, recv_sem, hop_send, hop_recv):
    count = lax.axis_size("tile")
    core, col, row = place(lax.axis_index("tile"), across)

    def hop(k, source, target, tile):
        return pltpu.make_async_remote_copy(
            src_ref=source, dst_ref=target, send_sem=hop_send.at[k], recv_sem=hop_recv.at[k],
            device_id={"tile": tile}, device_id_type=MESH)

    def fill_extra(e, carry):
        block = jnp.where(second_valid[0, e] > 0, blocks[second_ids[0, e]], 0.0)
        extra[e // (across * rows), e // rows % across, e % rows] = block.astype(extra.dtype)
        return carry

    def fill_direct(t, carry):
        direct[t] = blocks[ids[0, t]].astype(direct.dtype)
        return carry

    lax.fori_loop(0, count, fill_extra, 0)
    lax.fori_loop(0, count, fill_direct, 0)
    greet("tile")
    first = hop(0, extra.at[1 - core], near, (row * across + col) * 2 + 1 - core)
    first.start()
    start_direct(1, count // 2, direct, got, send_sem, recv_sem)
    own = keep_own(direct, got, own_sem)
    first.wait()
    near_sum[...] = extra[core] + near[...]
    hops = []
    for k in range(1, across):
        to = lax.rem(col + k, across)
        hops.append(hop(k, near_sum.at[to], run.at[k - 1], (row * across + to) * 2 + core))
        hops[-1].start()
    start_direct(count // 2, count, direct, got, send_sem, recv_sem)
    for copy in hops:
        copy.wait()
    total = near_sum[col]
    for k in range(across - 1):
        total = total + run[k]
    run_sum[...] = total
    hops = []
    for k in range(1, rows):
        to = lax.rem(row + k, rows)
        hops.append(hop(across - 1 + k, run_sum.at[to], far.at[k - 1], (to * across + col) * 2 + core))
        hops[-1].start()
    for copy in hops:
        copy.wait()
    total = run_sum[row]
    for k in range(rows - 1):
        total = total + far[k]
    got[count] = total
    own.wait()
    wait_direct(direct, got, send_sem, recv_sem)


def return_kernel(across, rows, direct, extra, got,
                  own_sem, send_sem, recv_sem, hop_send, hop_recv):
    count = lax.axis_size("tile")
    core, col, row = place(lax.axis_index("tile"), across)
    half = across * rows

    def hop(k, source, target, tile):
        return pltpu.make_async_remote_copy(
            src_ref=source, dst_ref=target, send_sem=hop_send.at[k], recv_sem=hop_recv.at[k],
            device_id={"tile": tile}, device_id_type=MESH)

    greet("tile")
    base = count + core * half + col * rows
    mine = pltpu.make_async_copy(extra, got.at[base + row], hop_send.at[across + rows - 1])
    mine.start()
    hops = []
    for k in range(1, rows):
        to = lax.rem(row + k, rows)
        hops.append(hop(k, extra, got.at[base + row], (to * across + col) * 2 + core))
        hops[-1].start()
    start_direct(1, count // 2, direct, got, send_sem, recv_sem)
    own = keep_own(direct, got, own_sem)
    mine.wait()
    for copy in hops:
        copy.wait()
    hops = []
    for k in range(1, across):
        to = lax.rem(col + k, across)
        part = got.at[pl.ds(base, rows)]
        hops.append(hop(rows - 1 + k, part, part, (row * across + to) * 2 + core))
        hops[-1].start()
    start_direct(count // 2, count, direct, got, send_sem, recv_sem)
    for copy in hops:
        copy.wait()
    part = got.at[pl.ds(count + core * half, half)]
    last = hop(0, part, part, (row * across + col) * 2 + 1 - core)
    last.start()
    last.wait()
    own.wait()
    wait_direct(direct, got, send_sem, recv_sem)


def chips_of(count):
    across = 4 if count % 8 == 0 else 1
    return across, count // (2 * across)


def by_core(values):
    across, rows = chips_of(values.shape[0])
    values = values.reshape(rows, across, 2, *values.shape[1:])
    return jnp.swapaxes(values, 0, 2)


def exchange_sems(count, across, rows):
    dma = pltpu.SemaphoreType.DMA
    return [dma, dma((count,)), dma((count,)), dma((across + rows,)), dma((across + rows,))]


def fetch(blocks, ids, second_ids, second_valid):
    high, wide = blocks.shape[1:]
    count = ids.shape[0]
    scalars = [x.reshape(1, count).astype(jnp.int32) for x in (ids, second_ids, second_valid)]
    across, rows = chips_of(count)
    smem = pl.BlockSpec(memory_space=pltpu.SMEM)
    vmem = pl.BlockSpec(memory_space=pltpu.VMEM)
    buffer = lambda *dims: pltpu.VMEM((*dims, high, wide), jnp.bfloat16)
    return pl.pallas_call(
        lambda *refs: fetch_kernel(across, rows, *refs),
        out_shape=jax.ShapeDtypeStruct((count + 1, high, wide), jnp.bfloat16),
        in_specs=[smem, smem, smem, vmem],
        out_specs=vmem,
        scratch_shapes=[
            buffer(count), buffer(2, across, rows),
            buffer(across, rows), buffer(across, rows), buffer(across - 1, rows),
            buffer(rows), buffer(rows - 1), *exchange_sems(count, across, rows)],
        compiler_params=pltpu.CompilerParams(collective_id=1, has_side_effects=True),
        name="fetch",
    )(*scalars, blocks)


def give_back(direct, extra):
    count, high, wide = direct.shape
    across, rows = chips_of(count)
    vmem = pl.BlockSpec(memory_space=pltpu.VMEM)
    return pl.pallas_call(
        lambda *refs: return_kernel(across, rows, *refs),
        out_shape=jax.ShapeDtypeStruct((2 * count, high, wide), direct.dtype),
        in_specs=[vmem, vmem],
        out_specs=vmem,
        scratch_shapes=exchange_sems(count, across, rows),
        compiler_params=pltpu.CompilerParams(collective_id=2, has_side_effects=True),
        name="give_back",
    )(direct, extra)


def angle_kernel(parts, out, landed, partial, other,
                 in_send, in_recv, pair_send, pair_recv, right_send, right_recv, left_send, left_recv):
    ring = parts.shape[0]
    me = lax.axis_index("angle")
    spot, side = me // 2, me % 2

    def copy(source, target, send_sem, recv_sem, to, at):
        return pltpu.make_async_remote_copy(
            src_ref=source, dst_ref=target, send_sem=send_sem, recv_sem=recv_sem,
            device_id={"angle": to * 2 + at}, device_id_type=MESH)

    barrier = pltpu.get_barrier_semaphore()
    for k in range(1, ring):
        pl.semaphore_signal(barrier, inc=1, device_id={"angle": lax.rem(spot + k, ring) * 2 + side},
                            device_id_type=MESH)
    pl.semaphore_signal(barrier, inc=1, device_id={"angle": spot * 2 + 1 - side}, device_id_type=MESH)
    pl.semaphore_wait(barrier, ring)

    copies = []
    for k in range(1, ring):
        to = lax.rem(spot + k, ring)
        copies.append(copy(parts.at[to], landed.at[k - 1], in_send.at[k - 1], in_recv.at[k - 1], to, side))
        copies[-1].start()
    for c in copies:
        c.wait()
    total = parts[spot].astype(jnp.float32)
    for k in range(ring - 1):
        total = total + landed[k].astype(jnp.float32)
    partial[...] = total
    pair = copy(partial, other, pair_send, pair_recv, spot, 1 - side)
    pair.start()
    pair.wait()
    out[spot] = partial[...] + other[...]
    right, left = lax.rem(spot + 1, ring), lax.rem(spot + ring - 1, ring)
    far = ring // 2
    reach = ((far, ring - 1 - far), (ring - 1 - far, far))

    def to_right(j, step):
        block = out.at[lax.rem(spot + ring - step, ring), j]
        return copy(block, block, right_send.at[j, step], right_recv.at[j, step], right, side)

    def to_left(j, step):
        block = out.at[lax.rem(spot + step, ring), j]
        return copy(block, block, left_send.at[j, step], left_recv.at[j, step], left, side)

    def from_left(j, step):
        block = out.at[lax.rem(spot + ring - step - 1, ring), j]
        return copy(block, block, right_send.at[j, step], right_recv.at[j, step], right, side)

    def from_right(j, step):
        block = out.at[lax.rem(spot + step + 1, ring), j]
        return copy(block, block, left_send.at[j, step], left_recv.at[j, step], left, side)

    sent = []
    for j in range(2):
        sent += [to_right(j, 0), to_left(j, 0)]
        sent[-2].start()
        sent[-1].start()
    for step in range(far):
        for j in range(2):
            if step < reach[j][0]:
                from_left(j, step).wait_recv()
                if step + 1 < reach[j][0]:
                    sent.append(to_right(j, step + 1))
                    sent[-1].start()
            if step < reach[j][1]:
                from_right(j, step).wait_recv()
                if step + 1 < reach[j][1]:
                    sent.append(to_left(j, step + 1))
                    sent[-1].start()
    for c in sent:
        c.wait_send()


def sum_over_angle(parts):
    angles, high, wide = parts.shape
    ring = angles // 2
    vmem = pl.BlockSpec(memory_space=pltpu.VMEM)
    dma = pltpu.SemaphoreType.DMA
    ring_sems = dma((2, ring))
    out = pl.pallas_call(
        angle_kernel,
        out_shape=jax.ShapeDtypeStruct((ring, 2, high, wide), jnp.float32),
        in_specs=[vmem],
        out_specs=vmem,
        scratch_shapes=[
            pltpu.VMEM((ring - 1, 2, high, wide), parts.dtype),
            pltpu.VMEM((2, high, wide), jnp.float32),
            pltpu.VMEM((2, high, wide), jnp.float32),
            dma((ring - 1,)), dma((ring - 1,)), dma, dma,
            ring_sems, ring_sems, ring_sems, ring_sems],
        compiler_params=pltpu.CompilerParams(collective_id=3, has_side_effects=True),
        name="angle_sum",
    )(parts.reshape(ring, 2, high, wide))
    return out.reshape(angles, high, wide)


def adam_update(params, moment_one, moment_two, gradient):
    fresh_one = BETA_FIRST * moment_one + (1.0 - BETA_FIRST) * gradient
    fresh_two = BETA_SECOND * moment_two + (1.0 - BETA_SECOND) * gradient * gradient
    fresh_params = params - STEP_SIZE * fresh_one / (jnp.sqrt(fresh_two) + EPSILON)
    return (fresh_params, fresh_one, fresh_two)


def per_device(
    volume,
    first_moment,
    second_moment,
    probe,
    measured,
    scan_rows,
    scan_cols,
    owner_ids,
    block_ids,
    interp_weights,
):
    tile_index = lax.axis_index("tile")
    tile_count = lax.axis_size("tile")
    block_count = volume.shape[0]
    block_rows = volume.shape[2]
    slab_width = volume.shape[3]
    probe_size = probe.shape[1]
    margin = probe_size // 2
    requests = owner_ids.shape[2]
    row_blocks = interp_weights.shape[2]
    per_slice = slab_width // block_rows
    layers = row_blocks // per_slice
    group_owner = owner_ids[0]
    group_block = block_ids[0]
    request_slots = jnp.arange(requests, dtype=jnp.int32)
    my_owner = lax.dynamic_index_in_dim(group_owner, tile_index, 0, keepdims=False)
    earlier = request_slots[None, :] < request_slots[:, None]
    my_rank = jnp.sum((my_owner[:, None] == my_owner[None, :]) & earlier, axis=1)
    mine = group_owner == tile_index
    first_slot = jnp.min(jnp.where(mine, request_slots, requests), axis=1)
    last_slot = jnp.max(jnp.where(mine, request_slots, -1), axis=1)
    slots = jnp.stack([first_slot, last_slot], axis=1)
    send_valid = jnp.stack([last_slot >= 0, last_slot > first_slot], axis=1)
    chosen = slots[:, :, None] == request_slots[None, None, :]
    send_block = jnp.sum(jnp.where(chosen, group_block[:, None, :], 0), axis=2)
    weight = interp_weights[0, 0]
    complement = 1.0 - weight
    block_size = (2 * block_rows, slab_width)
    incoming = fetch(
        volume.reshape(block_count, *block_size),
        send_block[:, 0],
        by_core(send_block[:, 1]),
        by_core(send_valid[:, 1]),
    )
    fetched = (
        incoming[jnp.where(my_rank == 0, my_owner, tile_count)]
        .astype(jnp.float32)
        .reshape(row_blocks, 2, 2, block_rows, slab_width)
    )
    obj_rows = (
        weight[:, None, None, None] * fetched[:, 0]
        + complement[:, None, None, None] * fetched[:, 1]
    )
    object_tile = obj_rows.reshape(layers, per_slice, 2, block_rows, slab_width).transpose(
        0, 2, 1, 3, 4
    )
    object_tile = object_tile.reshape(layers, 2, slab_width, slab_width).astype(jnp.bfloat16)
    object_tile = object_tile.reshape(layers * 2, slab_width, slab_width)
    before = from_behind(object_tile[..., slab_width - margin :], "tile", 1)
    after = from_behind(object_tile[..., :margin], "tile", -1)
    interior, low_edge, high_edge = local_gradient(
        object_tile, before, after, probe, scan_rows[0, 0], scan_cols[0, 0], measured[0, 0]
    )
    from_left = from_behind(high_edge, "tile", 1).astype(jnp.float32)
    from_right = from_behind(low_edge, "tile", -1).astype(jnp.float32)
    middle = jnp.zeros((layers * 2, slab_width, slab_width - 2 * margin), jnp.float32)
    interior = interior + jnp.concatenate([from_left, middle, from_right], axis=2)
    grad_rows = interior.reshape(layers, 2, per_slice, block_rows, slab_width).transpose(
        0, 2, 1, 3, 4
    )
    grad_rows = grad_rows.reshape(row_blocks, 2, block_rows, slab_width)
    request_grads = jnp.stack(
        [weight[:, None, None, None] * grad_rows, complement[:, None, None, None] * grad_rows],
        axis=1,
    )
    request_grads = request_grads.reshape(requests, *block_size).astype(jnp.bfloat16)
    owner_range = jnp.arange(tile_count, dtype=jnp.int32)
    first_of = (my_owner[None, :] == owner_range[:, None]) & (my_rank[None, :] == 0)
    back_index = jnp.sum(jnp.where(first_of, request_slots[None, :], 0), axis=1)
    second = jnp.sum(jnp.where(my_rank == 1, request_slots, 0))
    arrived = give_back(
        request_grads[back_index],
        lax.dynamic_index_in_dim(request_grads, second, 0, keepdims=False),
    )
    selector = (
        send_block[:, :, None] == jnp.arange(block_count, dtype=jnp.int32)[None, None, :]
    ) & send_valid[:, :, None]
    selector = jnp.concatenate(
        [selector[:, 0], by_core(selector[:, 1]).reshape(tile_count, block_count)], axis=0
    ).astype(jnp.bfloat16)
    grad_volume = jnp.einsum(
        "nb,nhw->bhw", selector, arrived, preferred_element_type=jnp.float32
    )
    rows_total = block_count * 2 * block_rows
    angles = lax.axis_size("angle")
    partial_sums = grad_volume.reshape(angles, rows_total // angles, slab_width)
    gradient = sum_over_angle(partial_sums.astype(jnp.bfloat16)).reshape(volume.shape)
    return adam_update(volume, first_moment, second_moment, gradient)


def solution(mesh):
    in_specs = (
        P("tile", None, None, None),
        P("tile", None, None, None),
        P("tile", None, None, None),
        P(),
        P("angle", "tile", None, None, None),
        P("angle", "tile", None),
        P("angle", "tile", None),
        P("angle", None, None),
        P("angle", None, None),
        P("angle", "tile", None),
    )
    out_specs = (
        P("tile", None, None, None),
        P("tile", None, None, None),
        P("tile", None, None, None),
    )
    return jax.shard_map(
        per_device, mesh=mesh, in_specs=in_specs, out_specs=out_specs, check_vma=False
    )
```
